128 devices in a mesh: gx: 8 (over x, core), yz: 16 (over y, z).
Axes of the slice: x: 4, y: 4, z: 4, core: 2. Of those that a mesh axis runs over, the one named last changes fastest.
Arguments:
- ref_pos: float32 [4096, 3, 128], P(('gx', 'yz')), may hold values from 0 to 1
- disp: float32 [4096, 3, 128], P(('gx', 'yz')), may hold values from -1.2 to 1.2
- volume: float32 [4096, 128], P(('gx', 'yz')), may hold values from 0.5 to 2
- lame: float32 [4096, 2, 128], P(('gx', 'yz')), may hold values from 0.3 to 3
- pad_count: int32 [4096], P(('gx', 'yz')), may hold values from 0 to 63
- nbr_owner: int32 [4096, 8, 1], P(('gx', 'yz')), may hold values from 0 to 127; in each aligned block of 256 rows (0 to 255, 256 to 511, ..., all dimensions but the last counted through in order) at most 4 rows name the same one
- nbr_local: int32 [4096, 8], P(('gx', 'yz')), may hold values from 0 to 31
- contact_block: int32 [4096, 2], P(('gx', 'yz')), may hold values from 0 to 4095, as said below
Outputs:
- force: float32 [4096, 3, 128], P(('gx', 'yz'))
- piola: float32 [4096, 9, 128], P(('gx', 'yz'))
The draws below stay inside these ranges and needn't reach their ends.
Inputs may be any that keep to these rules, and one draw needn't show every extreme that they name: `nbr_owner`: among the 256 entries of one device's blocks no owner device is named more than 4 times; in every draw some device names some owner exactly 4 times. `contact_block`: each entry names one of the last 4 blocks of the device one step lower along gx with the same yz index, or one of the first 4 blocks of the device one step higher along gx with the same yz index.
All inputs are finite; a program needn't handle non-finite values.
Results may differ from the reference program's by a relative error of at most 0.0003.
Values sent between devices are 32-bit elements; how exact they have to be, the bound alone decides.
No kernel may reach another device: no remote copies, remote signals or barrier semaphores. Data moves between devices by JAX's collectives and lax.ppermute only.
A program may use at most 64 MiB of HBM per device.

```python
import math
import jax
import jax.numpy as jnp
import numpy as np
from jax import lax

BLK = 128
NB = 32
K = 8
KC = 2
SH = 4
NBLOCKS = 4096
CAP = 4
N_GX = 8
N_YZ = 16
DEVICES = 128


def draw_contact_block(key, part):
    block_ids = jnp.arange(NBLOCKS)
    device = block_ids // NB
    slab_row = device // N_YZ
    column = device % N_YZ
    side_key, pick_key = jax.random.split(jax.random.fold_in(key, 17))
    upward = jax.random.randint(side_key, (NBLOCKS, KC), 0, 2)
    upward = jnp.where(slab_row[:, None] == 0, 1, jnp.where(slab_row[:, None] == N_GX - 1, 0, upward))
    offset = jax.random.randint(pick_key, (NBLOCKS, KC), 0, SH)
    local_row = jnp.where(upward == 1, offset, NB - SH + offset)
    target = slab_row[:, None] + 2 * upward - 1
    return ((target * N_YZ + column[:, None]) * NB + local_row).astype(jnp.int32)


def with_ends(values, rng, least, top_value):
    index_at = [jax.random.randint(jax.random.fold_in(rng, axis), (), 0, length) for axis, length in enumerate(values.shape)]
    longest = values.shape.index(max(values.shape))
    next_to = index_at[:longest] + [(index_at[longest] + 1) % values.shape[longest]] + index_at[longest + 1:]
    return values.at[tuple(index_at)].set(least).at[tuple(next_to)].set(top_value)


def level_of(rng, dims, cuts, smallest, high):
    factor_of, own = 1.0, jax.random.fold_in(rng, 6)
    for position, parts in cuts:
        heights = jnp.exp(jax.random.uniform(jax.random.fold_in(own, position), (parts,), jnp.float32, smallest / len(cuts), high / len(cuts)))
        factor_of = factor_of * jnp.repeat(heights, dims[position] // parts).reshape([-1 if axis == position else 1 for axis in range(len(dims))])
    return factor_of


def shared_out(key, own, number, rows, number_of, top, most, skew):
    ranking = jax.random.permutation(key, number_of)
    crowded, ordinary = load_shares(number_of, rows * top, most, skew, True), load_shares(number_of, rows * top, most, skew, False)
    places = jnp.arange(number_of)

    def named(sizes, rotation):
        used = int((sizes > 0).sum())
        fixed = max(1, used // 4)
        passed = fixed + (places - fixed + rotation * (used - fixed)) % max(1, number_of - fixed)
        return jnp.zeros((number_of,), jnp.int32).at[ranking[jnp.where(places < fixed, places, passed)]].set(jnp.asarray(sizes, jnp.int32))

    sizes = jnp.where(number % 4 == 0, named(crowded, number // 4), named(ordinary, number - number // 4 - 1))
    mixed = jax.random.permutation(jax.random.fold_in(own, 3), number_of)
    donor, sink = mixed[0:number_of // 2 * 2:2], mixed[1:number_of // 2 * 2:2]
    slack = jnp.minimum(sizes[donor] - 1, most - sizes[sink]) // 2
    slack = jnp.where((donor == ranking[0]) | (sink == ranking[0]) | (sizes[sink] == 0), 0, jnp.maximum(slack, 0))
    passed = jax.random.randint(jax.random.fold_in(own, 4), (number_of // 2,), 0, 1 << 20) % (slack + 1)
    sizes = sizes.at[donor].add(-passed).at[sink].add(passed)
    members = jnp.searchsorted(jnp.cumsum(sizes), jnp.arange(rows * top), side="right").astype(jnp.int32)
    table = members.reshape(top, rows).T
    table = table[jax.random.permutation(jax.random.fold_in(own, 1), rows)]
    rotation = jax.random.randint(jax.random.fold_in(own, 2), (rows, 1), 0, top)
    return jnp.take_along_axis(table, (jnp.arange(top)[None, :] + rotation) % top, axis=1)


def load_shares(count, total, most, lean, full):
    loads = [(1 << 20) // math.isqrt(grade ** lean) + 1 for grade in range(1, count + 1)]
    largest = most if full else min(most, max(-(-total // count), total * loads[0] // sum(loads)))
    least = 1 if total - largest >= count - 1 else 0
    holding, rest = [largest] + [least] * (count - 1), total - largest - least * (count - 1)
    while rest > 0:
        free = [i for i in range(1, count) if holding[i] < largest] or [i for i in range(1, count) if holding[i] < most]
        mass, budget = sum([loads[i] for i in free]), rest
        for i in free:
            more = min(most - holding[i], max(1, budget * loads[i] // mass), rest)
            holding[i] = holding[i] + more
            rest = rest - more
    return np.array(holding)


def gaussian(stream_key, extent, scale, limit, cuts=(), kind=jnp.bfloat16):
    result = scale * jax.random.normal(stream_key, extent, jnp.float32)
    if cuts:
        result = result * level_of(stream_key, extent, cuts, -0.22, 0.18)
    return jnp.clip(result, -limit, limit).astype(kind)


def setup_inputs(seed: int = 0) -> dict:
    keys = jax.random.split(jax.random.key(seed), 9)
    ref_pos = jnp.clip(1.0 * jax.random.uniform(keys[0], (NBLOCKS, 3, BLK), jnp.float32) ** level_of(keys[0], (NBLOCKS, 3, BLK), ((0, 128),), -0.2, 0.2), 0.0, 1.0)
    disp = gaussian(keys[1], (NBLOCKS, 3, BLK), 0.3, 1.2, ((0, 128),), jnp.float32)
    volume = jnp.clip(jnp.exp(math.log(2.0) - 1.3862944 * jax.random.uniform(keys[2], (NBLOCKS, BLK), jnp.float32) ** level_of(keys[2], (NBLOCKS, BLK), ((0, 128),), -0.2, 0.2)), 0.5, 2.0)
    lame = jnp.clip(jnp.exp(math.log(3.0) - 2.3025851 * jax.random.uniform(keys[3], (NBLOCKS, 2, BLK), jnp.float32) ** level_of(keys[3], (NBLOCKS, 2, BLK), ((0, 128),), -0.2, 0.2)), 0.3, 3.0)
    pad_count = with_ends(jax.random.randint(keys[4], (NBLOCKS,), 0, BLK // 2), jax.random.fold_in(keys[4], 1), 0, (BLK // 2) - 1).astype(jnp.int32)
    nbr_owner_keys = jax.random.split(jax.random.fold_in(keys[5], 1), NBLOCKS * K // (NB * K))
    nbr_owner_turns = jax.random.permutation(jax.random.fold_in(keys[5], 3), NBLOCKS * K // (NB * K))
    nbr_owner = jax.vmap(lambda own, number: shared_out(jax.random.fold_in(keys[5], 2), own, number, NB * K, DEVICES, 1, CAP, 2))(nbr_owner_keys, nbr_owner_turns).reshape((NBLOCKS, K, 1))
    nbr_local = with_ends(jax.random.randint(keys[6], (NBLOCKS, K), 0, NB), jax.random.fold_in(keys[6], 1), 0, NB - 1).astype(jnp.int32)
    contact_block = draw_contact_block(jax.random.fold_in(keys[8], 71), 0)
    return {"ref_pos": ref_pos, "disp": disp, "volume": volume, "lame": lame, "pad_count": pad_count, "nbr_owner": nbr_owner, "nbr_local": nbr_local, "contact_block": contact_block}


support_sq = 0.5
contact_sq = 0.1
penalty = 200.0
group_blocks = 4
highest = lax.Precision.HIGHEST

def block_terms(own_data, lame_block, neighbours, partners):
    block_len = own_data.shape[-1]
    fanout = neighbours.shape[0]
    identity = jnp.eye(3, dtype=own_data.dtype)[:, :, None]
    anchor = own_data[0:3]
    moved = own_data[3:6]
    weight = own_data[6]
    inside = (weight > 0).astype(own_data.dtype)
    offset = anchor[:, None, :, None] - jnp.transpose(neighbours[:, 0:3], (1, 0, 2))[:, :, None, :]
    radius = lax.optimization_barrier(jnp.sum(offset * offset, axis=0))
    kernel = jnp.square(jnp.maximum(1.0 - radius / support_sq, 0.0))
    slope = -3.0 / math.sqrt(fanout * block_len) * kernel[None] * offset
    far_weight = neighbours[:, 6]
    column = jnp.einsum('ckij,kj->ci', slope, far_weight, precision=highest)
    spread = jnp.einsum('ckij,kaj->aci', slope, far_weight[:, None, :] * neighbours[:, 3:6], precision=highest)
    deform = identity + spread - moved[:, None, :] * column[None, :, :]
    strain = 0.5 * (jnp.einsum('cai,cbi->abi', deform, deform, precision=highest) - identity)
    trace = strain[0, 0] + strain[1, 1] + strain[2, 2]
    second = lame_block[0] * trace * identity + 2.0 * lame_block[1] * strain
    piola = jnp.einsum('aci,cbi->abi', deform, second, precision=highest) * inside
    own_force = weight * jnp.einsum('abi,bi->ai', piola, column, precision=highest)
    returned_part = -far_weight[:, None, :] * jnp.einsum('bkij,abi->kaj', slope, weight * piola, precision=highest)
    current = anchor + moved
    separation = current[:, None, :, None] - jnp.transpose(partners[:, 0:3], (1, 0, 2))[:, :, None, :]
    intersection = jnp.square(jnp.maximum(contact_sq - lax.optimization_barrier(jnp.sum(separation * separation, axis=0)), 0.0))
    contact_push = penalty * inside * jnp.einsum('ckij,kj->ci', separation * intersection[None], partners[:, 3], precision=highest)
    return (piola.reshape(9, block_len), own_force + contact_push, returned_part)

def reference(ref_pos, disp, volume, lame, pad_count, nbr_owner, nbr_local, contact_block):
    usable = (jnp.arange(BLK)[None, :] < (BLK - pad_count)[:, None]).astype(ref_pos.dtype)
    weight = volume * usable
    packed = jnp.concatenate([ref_pos, disp, weight[:, None, :]], axis=1)
    surface = jnp.concatenate([ref_pos + disp, weight[:, None, :]], axis=1)
    nbr_id = (nbr_owner[:, :, 0] * NB + nbr_local).astype(jnp.int32)
    groups = NBLOCKS // group_blocks

    def split_up(array):
        return array.reshape((groups, group_blocks) + array.shape[1:])

    def one_group(carry, inputs):
        own_data, lame_group, wanted_ids, contact_ids = inputs
        piola, forces, returned_part = jax.vmap(block_terms)(own_data, lame_group, packed[wanted_ids], surface[contact_ids])
        carry = carry.at[wanted_ids.reshape(-1)].add(returned_part.reshape(-1, 3, BLK))
        return (carry, (piola, forces))
    returned, (piola, forces) = lax.scan(one_group, jnp.zeros_like(ref_pos), (split_up(packed), split_up(lame), split_up(nbr_id), split_up(contact_block.astype(jnp.int32))))
    return (forces.reshape(NBLOCKS, 3, BLK) + returned, piola.reshape(NBLOCKS, 9, BLK))
```

```python
import functools
import math

import jax
import jax.numpy as jnp
from jax import lax
from jax.experimental import pallas as pl
from jax.experimental.pallas import tpu as pltpu
from jax.sharding import PartitionSpec as P

SH = 4
SUPPORT_SQ = 0.5
CONTACT_SQ = 0.1
PENALTY = 200.0
GROUP = 8
ROWS = 7
F32 = jnp.float32
BF16 = jnp.bfloat16
AXES = ("gx", "yz")
NT = (((1,), (1,)), ((), ()))
NN = (((1,), (0,)), ((), ()))


def high(x):
    return x.astype(BF16).astype(F32)


def parts(x, count):
    out = []
    for _ in range(count - 1):
        h = high(x)
        out.append(h)
        x = x - h
    out.append(high(x))
    return out


def mm(a, b, dims):
    return lax.dot_general(a, b, dims, preferred_element_type=F32)


def contact_kernel(pos_ref, disp_ref, mask_ref, shell_ref, pick_ref, out_ref, wide, cur):
    blocks, lanes = mask_ref.shape
    count = shell_ref.shape[0]
    for c in range(3):
        cur[c] = pos_ref[c] + disp_ref[c]
    for s in range(count):
        turned = jnp.transpose(jnp.concatenate([shell_ref[s], shell_ref[s]], axis=0))
        for c in range(4):
            wide[s, c] = jnp.broadcast_to(turned[:, c : c + 1], (lanes, lanes))

    def block(b, _):
        own = [jnp.broadcast_to(cur[c, pl.ds(b, 1), :], (8, lanes)) for c in range(3)]
        total = [jnp.zeros((8, lanes), F32) for _ in range(3)]
        for k in range(2):
            s = pick_ref[b, k]
            for r in range(lanes // 8):
                rows = pl.ds(r * 8, 8)
                gap = [own[c] - wide[s, c, rows, :] for c in range(3)]
                near = jnp.maximum(
                    CONTACT_SQ - (gap[0] * gap[0] + gap[1] * gap[1] + gap[2] * gap[2]), 0.0
                )
                push = near * near * wide[s, 3, rows, :]
                total = [total[c] + push * gap[c] for c in range(3)]
        scale = PENALTY * mask_ref[pl.ds(b, 1), :]
        for c in range(3):
            out_ref[c, pl.ds(b, 1), :] = scale * jnp.sum(total[c], axis=0, keepdims=True)
        return 0

    lax.fori_loop(0, blocks, block, 0)


def main_kernel(
    slot_ref, pos_ref, disp_ref, weight_ref, lame_ref, contact_ref, got_ref,
    piola_ref, force_ref, back_ref,
    pick, far, bs, fs, a_s, at, b_all, f_all, k_hi, k_lo, ss, gs, ts,
):
    blocks, lanes = weight_ref.shape
    fanout = far.shape[2]
    wide = fanout * lanes
    coeff = -3.0 / math.sqrt(wide)
    inv = 1.0 / SUPPORT_SQ
    back_ref[...] = jnp.zeros_like(back_ref)
    ones = jnp.ones((8, lanes), F32)
    zero = jnp.zeros((8, lanes), F32)
    for f in range(21, 32):
        bs[pl.ds(f, 8, stride=32), :] = ones if f < 24 else zero
    for f in range(18, 32):
        a_s[pl.ds(f, 8, stride=32), :] = ones if f < 21 else zero
    for f in range(12, 32):
        if f < 16 or f >= 28:
            gs[pl.ds(f, 8, stride=32), :] = zero

    def own_side(g, _):
        start = pl.multiple_of(g * GROUP, GROUP)
        rows = pl.ds(start, GROUP)
        near = [pos_ref[c, rows, :] for c in range(3)]
        near = [x - x[:, 0:1] for x in near]
        norm = near[0] * near[0] + near[1] * near[1] + near[2] * near[2]
        for c in range(3):
            h, m, l = [2.0 * inv * p for p in parts(near[c], 3)]
            for f, v in ((0, h), (3, h), (6, m), (9, m), (12, h), (15, l)):
                a_s[pl.ds(f + c, 8, stride=32), :] = v
        for f, v in enumerate(parts(1.0 - inv * norm, 3)):
            a_s[pl.ds(21 + f, 8, stride=32), :] = v
        for q in range(GROUP):
            at[start + q] = jnp.transpose(a_s[pl.ds(q * 32, 32), :]).astype(BF16)
        return 0

    lax.fori_loop(0, blocks // GROUP, own_side, 0)

    def far_side(b, _):
        for k in range(fanout):
            first = slot_ref[b * fanout + k] * ROWS
            for c in range(ROWS):
                pick[c, pl.ds(k, 1), :] = got_ref[pl.ds(first + c, 1), :]
        there = [pick[c] - pos_ref[c, pl.ds(b, 1), 0:1] for c in range(3)]
        moved = [pick[3 + c] for c in range(3)]
        weight = pick[6]
        for c in range(3):
            far[b, c] = there[c]
        far[b, 3] = weight
        norm = there[0] * there[0] + there[1] * there[1] + there[2] * there[2]
        for c in range(3):
            h, m, l = parts(there[c], 3)
            for f, v in ((0, h), (3, m), (6, h), (9, m), (12, l), (15, h)):
                bs[pl.ds(f + c, 8, stride=32), :] = v
        for f, v in enumerate(parts(-inv * norm, 3)):
            bs[pl.ds(18 + f, 8, stride=32), :] = v
        heavy = [weight * x for x in moved]
        feats = [weight] + [weight * x for x in there] + heavy
        feats += [h * x for h in heavy for x in there]
        for f, v in enumerate(feats):
            h, l = parts(v, 2)
            fs[pl.ds(f, 8, stride=32), :] = h
            fs[pl.ds(16 + f, 8, stride=32), :] = l
        for k in range(fanout):
            cols = pl.ds(k * lanes, lanes)
            b_all[b, :, cols] = bs[pl.ds(k * 32, 32), :].astype(BF16)
            f_all[b, :, cols] = fs[pl.ds(k * 32, 32), :].astype(BF16)
        return 0

    lax.fori_loop(0, blocks, far_side, 0)

    def group(g, _):
        start = pl.multiple_of(g * GROUP, GROUP)
        rows = pl.ds(start, GROUP)

        def forward(q, _):
            b = start + q
            near = jnp.maximum(mm(at[b], b_all[b], NN), 0.0)
            near = near * near
            hi = near.astype(BF16)
            lo = (near - hi.astype(F32)).astype(BF16)
            k_hi[q] = hi
            k_lo[q] = lo
            sums = mm(f_all[b], hi, NT)
            sums = sums[0:16] + sums[16:32] + mm(f_all[b, 0:16, :], lo, NT)
            ss[pl.ds(pl.multiple_of(q * 16, 16), 16), :] = sums
            return 0

        lax.fori_loop(0, GROUP, forward, 0, unroll=2)

        total = [ss[pl.ds(f, GROUP, stride=16), :] for f in range(16)]
        weight = weight_ref[rows, :]
        inside = (weight > 0).astype(F32)
        here = [pos_ref[c, rows, :] for c in range(3)]
        here = [x - x[:, 0:1] for x in here]
        moved = [disp_ref[c, rows, :] for c in range(3)]
        column = [coeff * (here[c] * total[0] - total[1 + c]) for c in range(3)]
        deform = [
            [
                (1.0 if a == c else 0.0)
                + coeff * (here[c] * total[4 + a] - total[7 + 3 * a + c])
                - moved[a] * column[c]
                for c in range(3)
            ]
            for a in range(3)
        ]
        strain = [[None] * 3 for _ in range(3)]
        for a in range(3):
            for c in range(a, 3):
                v = sum(deform[k][a] * deform[k][c] for k in range(3))
                strain[a][c] = strain[c][a] = 0.5 * (v - (1.0 if a == c else 0.0))
        trace = lame_ref[0, rows, :] * (strain[0][0] + strain[1][1] + strain[2][2])
        twice = 2.0 * lame_ref[1, rows, :]
        second = [
            [(trace if a == c else 0.0) + twice * strain[a][c] for c in range(3)] for a in range(3)
        ]
        scaled = [[None] * 3 for _ in range(3)]
        for a in range(3):
            for c in range(3):
                v = sum(deform[a][k] * second[k][c] for k in range(3)) * inside
                piola_ref[3 * a + c, rows, :] = v
                scaled[a][c] = weight * v
        feats = [scaled[a][c] for a in range(3) for c in range(3)]
        for a in range(3):
            own = sum(scaled[a][c] * column[c] for c in range(3))
            force_ref[a, rows, :] = own + contact_ref[a, rows, :]
            feats.append(sum(scaled[a][c] * here[c] for c in range(3)))
        for f, v in enumerate(feats):
            h, l = parts(v, 2)
            gs[pl.ds(f, 8, stride=32), :] = h
            gs[pl.ds(16 + f, 8, stride=32), :] = l

        def backward(q, _):
            b = start + q
            feat = gs[pl.ds(pl.multiple_of(q * 32, 32), 32), :].astype(BF16)
            sums = mm(feat, k_hi[q], NN)
            sums = sums[0:16] + sums[16:32] + mm(feat[0:16], k_lo[q], NN)
            for k in range(fanout):
                ts[pl.ds(k * 16, 16), :] = sums[:, k * lanes : (k + 1) * lanes]
            back = [ts[pl.ds(f, fanout, stride=16), :] for f in range(12)]
            there = [far[b, c] for c in range(3)]
            scale = -coeff * far[b, 3]
            for a in range(3):
                v = back[9 + a] - sum(there[c] * back[3 * a + c] for c in range(3))
                pick[a] = scale * v
            for k in range(fanout):
                first = slot_ref[b * fanout + k] * 3
                for a in range(3):
                    back_ref[pl.ds(first + a, 1), :] = pick[a, pl.ds(k, 1), :]
            return 0

        lax.fori_loop(0, GROUP, backward, 0)
        return 0

    lax.fori_loop(0, blocks // GROUP, group, 0)


def gather_sum_kernel(code_ref, got_ref, force_ref, out_ref):
    comps, blocks, lanes = force_ref.shape
    rows = got_ref.shape[0]
    target = lax.broadcasted_iota(jnp.int32, (comps * blocks, rows), 0)
    chosen = (target == code_ref[...]).astype(F32).astype(BF16)
    out = force_ref[...].reshape(comps * blocks, lanes)
    for part in parts(got_ref[...], 3):
        out = out + mm(chosen, part.astype(BF16), NN)
    out_ref[...] = out.reshape(comps, blocks, lanes)


def vmem(count):
    return [pl.BlockSpec(memory_space=pltpu.VMEM)] * count


SMEM = pl.BlockSpec(memory_space=pltpu.SMEM)


def per_device(ref_pos, disp, volume, lame, pad_count, nbr_owner, nbr_local, contact_block):
    blocks, _, lanes = ref_pos.shape
    fanout = nbr_local.shape[1]
    across = lax.axis_size("gx")
    deep = lax.axis_size("yz")
    devices = across * deep
    cap = 2 * blocks * fanout // devices
    slots_all = devices * cap
    usable = (jnp.arange(lanes)[None, :] < (lanes - pad_count)[:, None]).astype(F32)
    weight = volume * usable
    mask = (weight > 0).astype(F32)

    owners = nbr_owner[:, :, 0].reshape(-1)
    wanted = nbr_local.reshape(-1)
    position = jnp.arange(owners.shape[0])
    before = (owners[:, None] == owners[None, :]) & (position[:, None] > position[None, :])
    slots = owners * cap + jnp.sum(before.astype(jnp.int32), axis=1)
    requests = jnp.full((slots_all,), -1, jnp.int32).at[slots].set(wanted)
    slot_ids = lax.all_to_all(
        requests.reshape(devices, cap), AXES, split_axis=0, concat_axis=0, tiled=True
    )

    packed = jnp.concatenate([ref_pos, disp, weight[:, None, :]], axis=1)
    picked = packed[jnp.maximum(slot_ids, 0)].reshape(devices, ROWS, cap, lanes)
    got = lax.all_to_all(picked, AXES, split_axis=0, concat_axis=0, tiled=True)
    got = got.reshape(slots_all * ROWS, lanes)

    surface = jnp.concatenate([ref_pos + disp, weight[:, None, :]], axis=1)
    up = [(i, i + 1) for i in range(across - 1)]
    down = [(i + 1, i) for i in range(across - 1)]
    below = lax.ppermute(surface[blocks - SH :], "gx", up)
    above = lax.ppermute(surface[:SH], "gx", down)
    shell = jnp.concatenate([below, above], axis=0)
    local = contact_block % blocks
    row = contact_block // blocks // deep
    pick = jnp.where(row < lax.axis_index("gx"), local - (blocks - SH), SH + local)

    pos_t = jnp.transpose(ref_pos, (1, 0, 2))
    disp_t = jnp.transpose(disp, (1, 0, 2))
    lame_t = jnp.transpose(lame, (1, 0, 2))
    contact = pl.pallas_call(
        contact_kernel,
        out_shape=jax.ShapeDtypeStruct((3, blocks, lanes), F32),
        in_specs=vmem(4) + [SMEM],
        out_specs=vmem(1)[0],
        scratch_shapes=[
            pltpu.VMEM((2 * SH, 4, lanes, lanes), F32),
            pltpu.VMEM((3, blocks, lanes), F32),
        ],
        cost_estimate=pl.CostEstimate(flops=20_000_000, bytes_accessed=200_000, transcendentals=0),
        name="contact",
    )(pos_t, disp_t, mask, shell, pick)

    wide = fanout * lanes
    piola, force, back = pl.pallas_call(
        main_kernel,
        out_shape=(
            jax.ShapeDtypeStruct((9, blocks, lanes), F32),
            jax.ShapeDtypeStruct((3, blocks, lanes), F32),
            jax.ShapeDtypeStruct((slots_all * 3, lanes), F32),
        ),
        in_specs=[SMEM] + vmem(6),
        out_specs=tuple(vmem(3)),
        scratch_shapes=[
            pltpu.VMEM((8, fanout, lanes), F32),
            pltpu.VMEM((blocks, 4, fanout, lanes), F32),
            pltpu.VMEM((fanout * 32, lanes), F32),
            pltpu.VMEM((fanout * 32, lanes), F32),
            pltpu.VMEM((GROUP * 32, lanes), F32),
            pltpu.VMEM((blocks, lanes, 32), BF16),
            pltpu.VMEM((blocks, 32, wide), BF16),
            pltpu.VMEM((blocks, 32, wide), BF16),
            pltpu.VMEM((GROUP, lanes, wide), BF16),
            pltpu.VMEM((GROUP, lanes, wide), BF16),
            pltpu.VMEM((GROUP * 16, lanes), F32),
            pltpu.VMEM((GROUP * 32, lanes), F32),
            pltpu.VMEM((fanout * 16, lanes), F32),
        ],
        cost_estimate=pl.CostEstimate(
            flops=60_000_000, bytes_accessed=4_000_000, transcendentals=0
        ),
        name="pairs",
    )(slots, pos_t, disp_t, weight, lame_t, contact, got)

    received = lax.all_to_all(
        back.reshape(devices, 3, cap, lanes), AXES, split_axis=0, concat_axis=0, tiled=True
    )
    ids = slot_ids.reshape(-1, 1)
    code = jnp.where(ids >= 0, ids + blocks * jnp.arange(3)[None, :], -1).reshape(1, -1)
    force = pl.pallas_call(
        gather_sum_kernel,
        out_shape=jax.ShapeDtypeStruct((3, blocks, lanes), F32),
        in_specs=vmem(3),
        out_specs=vmem(1)[0],
        name="returned",
    )(code, received.reshape(slots_all * 3, lanes), force)
    return (jnp.transpose(force, (1, 0, 2)), jnp.transpose(piola, (1, 0, 2)))


def solution(mesh):
    return jax.shard_map(
        per_device,
        mesh=mesh,
        in_specs=(
            P(AXES, None, None),
            P(AXES, None, None),
            P(AXES, None),
            P(AXES, None, None),
            P(AXES),
            P(AXES, None, None),
            P(AXES, None),
            P(AXES, None),
        ),
        out_specs=(P(AXES, None, None), P(AXES, None, None)),
        check_vma=False,
    )
```

```python
import math

import jax
import jax.numpy as jnp
from jax import lax
from jax.experimental import pallas as pl
from jax.experimental.pallas import tpu as pltpu
from jax.sharding import PartitionSpec as P

SH = 4
SUPPORT_SQ = 0.5
CONTACT_SQ = 0.1
PENALTY = 200.0
GROUP = 8
ROWS = 7
SIDE = 48
F32 = jnp.float32
BF16 = jnp.bfloat16
AXES = ("gx", "yz")
NT = (((1,), (1,)), ((), ()))
NN = (((1,), (0,)), ((), ()))


def high(x):
    return x.astype(BF16).astype(F32)


def parts(x, count):
    out = []
    for _ in range(count - 1):
        h = high(x)
        out.append(h)
        x = x - h
    out.append(high(x))
    return out


def mm(a, b, dims):
    return lax.dot_general(a, b, dims, preferred_element_type=F32)


def plan_kernel(owner_ref, local_ref, ask_ref, start_ref, rows, *, cap):
    fanout, blocks = local_ref.shape
    devices, width = ask_ref.shape
    total = fanout * blocks
    for k in range(fanout):
        cols = pl.ds(k * blocks, blocks)
        rows[0:1, cols] = owner_ref[k]
        rows[1:2, cols] = local_ref[k : k + 1, :]
    owner = rows[0:1, :]
    local = (rows[1:2, :] + 1).astype(F32)
    named = owner == lax.broadcasted_iota(jnp.int32, (devices, total), 0)
    hot = named.astype(F32)
    earlier = lax.broadcasted_iota(jnp.int32, (total, total), 0) < lax.broadcasted_iota(
        jnp.int32, (total, total), 1
    )
    rank = mm(hot.astype(BF16), earlier.astype(F32).astype(BF16), NN)
    lane = lax.broadcasted_iota(jnp.int32, (width, total), 0)
    ask = jnp.zeros((devices, width), F32)
    for s in range(cap):
        chosen = jnp.where(rank == float(s), hot, 0.0).astype(BF16)
        ask = ask + mm(chosen, jnp.where(lane == s, local, 0.0).astype(BF16), NT)
    ask_ref[...] = ask.astype(jnp.int32) - 1
    place = jnp.sum(hot * rank, axis=0, keepdims=True).astype(jnp.int32)
    start_ref[0:1, :] = owner * (cap * ROWS) + place
    start_ref[1:2, :] = owner * (cap * 3) + place


def provide_kernel(ask_ref, pos_ref, disp_ref, weight_ref, out_ref, wide, *, cap):
    devices = ask_ref.shape[0]
    blocks, lanes = weight_ref.shape
    depth = 3 * blocks
    cols = []
    for c in range(ROWS):
        x = weight_ref[...] if c == 6 else (pos_ref if c < 3 else disp_ref)[c % 3]
        cols.append(jnp.concatenate(parts(x, 3), axis=0).astype(BF16))
    data = jnp.concatenate(cols, axis=1)
    for s in range(cap):
        wide[pl.ds(s, devices, stride=cap), :] = jnp.broadcast_to(
            ask_ref[:, s : s + 1], (devices, lanes)
        )
    step = 64
    local = lax.broadcasted_iota(jnp.int32, (step, depth), 1) % blocks
    for i in range(devices * cap // step):
        hot = (wide[pl.ds(i * step, step), 0:depth] == local).astype(F32).astype(BF16)
        got = mm(hot, data, NN)
        for j in range(step // cap):
            r = i * (step // cap) + j
            for c in range(ROWS):
                out_ref[pl.ds((r * ROWS + c) * cap, cap), :] = got[
                    j * cap : (j + 1) * cap, c * lanes : (c + 1) * lanes
                ]


def own_kernel(pos_ref, at_ref, centre_ref, side):
    _, blocks, lanes = pos_ref.shape
    inv = 1.0 / SUPPORT_SQ
    side[...] = jnp.zeros_like(side)
    centre_ref[...] = jnp.zeros_like(centre_ref)
    ones = jnp.ones((GROUP, lanes), F32)
    for d in (0, 3, 5):
        side[pl.ds(d * 8 + 7, GROUP, stride=SIDE), :] = ones

    def group(g, _):
        start = pl.multiple_of(g * GROUP, GROUP)
        norm = jnp.zeros((GROUP, lanes), F32)
        for c in range(3):
            x = pos_ref[c, pl.ds(start, GROUP), :]
            mid = jnp.broadcast_to(x[:, 0:1], x.shape)
            x = x - mid
            centre_ref[pl.ds(start * 8 + c, GROUP, stride=8), :] = mid
            norm = norm + x * x
            h, m, l = [2.0 * inv * p for p in parts(x, 3)]
            for d, v in enumerate((h, m, l, h, m, h)):
                side[pl.ds(d * 8 + c, GROUP, stride=SIDE), :] = v
        for d, v in enumerate(parts(1.0 - inv * norm, 3)):
            side[pl.ds(d * 8 + 3, GROUP, stride=SIDE), :] = v
        for q in range(GROUP):
            at_ref[start + q] = jnp.transpose(side[pl.ds(q * SIDE, SIDE), :]).astype(BF16)
        return 0

    lax.fori_loop(0, blocks // GROUP, group, 0)


def contact_kernel(pos_ref, disp_ref, weight_ref, below_ref, above_ref, pick_ref, out_ref, wide, cur):
    blocks, lanes = weight_ref.shape
    half = below_ref.shape[0]
    for c in range(3):
        cur[c] = pos_ref[c] + disp_ref[c]
    for s in range(2 * half):
        block = below_ref[s] if s < half else above_ref[s - half]
        turned = jnp.transpose(jnp.concatenate([block, block], axis=0))
        for c in range(4):
            wide[s, c] = jnp.broadcast_to(turned[:, c : c + 1], (lanes, lanes))

    def block(b, _):
        own = [jnp.broadcast_to(cur[c, pl.ds(b, 1), :], (8, lanes)) for c in range(3)]
        total = [jnp.zeros((8, lanes), F32) for _ in range(3)]
        for k in range(2):
            s = pick_ref[b, k]
            for r in range(lanes // 8):
                rows = pl.ds(r * 8, 8)
                gap = [own[c] - wide[s, c, rows, :] for c in range(3)]
                near = jnp.maximum(
                    CONTACT_SQ - (gap[0] * gap[0] + gap[1] * gap[1] + gap[2] * gap[2]), 0.0
                )
                push = near * near * wide[s, 3, rows, :]
                total = [total[c] + push * gap[c] for c in range(3)]
        scale = PENALTY * (weight_ref[pl.ds(b, 1), :] > 0).astype(F32)
        for c in range(3):
            out_ref[c, pl.ds(b, 1), :] = scale * jnp.sum(total[c], axis=0, keepdims=True)
        return 0

    lax.fori_loop(0, blocks, block, 0)


def main_kernel(
    start_ref, pos_ref, disp_ref, weight_ref, lame_ref, contact_ref, at_ref, centre_ref, got_ref,
    piola_ref, force_ref, back_ref,
    raw, far, b_all, f_all, k_all, ss, gs,
):
    blocks, lanes = weight_ref.shape
    fanout = far.shape[1]
    cap = 4
    coeff = -3.0 / math.sqrt(fanout * lanes)
    inv = 1.0 / SUPPORT_SQ
    back_ref[...] = jnp.zeros_like(back_ref)
    gs[...] = jnp.zeros_like(gs)
    raw[...] = jnp.zeros_like(raw)
    row = lax.broadcasted_iota(jnp.int32, (8, lanes), 0)

    def far_side(b, _):
        centre = centre_ref[pl.ds(pl.multiple_of(b * 8, 8), 8), :]
        for k in range(fanout):
            raw[k, 0:ROWS, :] = got_ref[pl.ds(start_ref[0, k * blocks + b], ROWS, stride=cap), :]
        for k in range(fanout):
            t = raw[k] - centre
            far[b, k] = t
            square = t * t
            norm = square[0:1] + square[1:2] + square[2:3]
            place = jnp.where(row == 3, 1.0, jnp.where(row == 7, -inv * norm, t))
            h, m, l = parts(place, 3)
            cols = pl.ds(k * lanes, lanes)
            b_all[b, :, cols] = jnp.concatenate([h, h, h, m, m, l], axis=0).astype(BF16)
            weight = t[6:7]
            plain = jnp.where(row == 6, 1.0, t)
            feats = [weight * plain] + [(weight * t[3 + a : 4 + a]) * plain for a in range(3)]
            split = [parts(v, 2) for v in feats]
            f_all[b, :, cols] = jnp.concatenate(
                [v[0] for v in split] + [v[1] for v in split], axis=0
            ).astype(BF16)
        return 0

    lax.fori_loop(0, blocks, far_side, 0, unroll=2)

    def group(g, _):
        start = pl.multiple_of(g * GROUP, GROUP)
        rows = pl.ds(start, GROUP)

        def forward(q, _):
            b = start + q
            sums = jnp.zeros((64, 2 * lanes), F32)
            for k in range(0, fanout, 2):
                cols = pl.ds(k * lanes, 2 * lanes)
                near = jnp.maximum(mm(at_ref[b], b_all[b, :, cols], NN), 0.0)
                near = near * near
                hi = near.astype(BF16)
                lo = (near - hi.astype(F32)).astype(BF16)
                both = jnp.concatenate([hi, lo], axis=0)
                k_all[q, :, cols] = both
                sums = sums + mm(f_all[b, :, cols], both, NT)
            sums = sums[:, 0:lanes] + sums[:, lanes:]
            ss[pl.ds(pl.multiple_of(q * 32, 32), 32), :] = sums[0:32] + sums[32:64]
            return 0

        lax.fori_loop(0, GROUP, forward, 0, unroll=4)

        def total(f):
            return ss[pl.ds(f, GROUP, stride=32), :]

        mass = total(6)
        weight = weight_ref[rows, :]
        inside = (weight > 0).astype(F32)
        here = [pos_ref[c, rows, :] for c in range(3)]
        here = [x - x[:, 0:1] for x in here]
        moved = [disp_ref[c, rows, :] for c in range(3)]
        column = [coeff * (here[c] * mass - total(c)) for c in range(3)]
        deform = [
            [
                (1.0 if a == c else 0.0)
                + coeff * (here[c] * total(3 + a) - total(8 + 8 * a + c))
                - moved[a] * column[c]
                for c in range(3)
            ]
            for a in range(3)
        ]
        strain = [[None] * 3 for _ in range(3)]
        for a in range(3):
            for c in range(a, 3):
                v = sum(deform[k][a] * deform[k][c] for k in range(3))
                strain[a][c] = strain[c][a] = 0.5 * (v - (1.0 if a == c else 0.0))
        trace = lame_ref[0, rows, :] * (strain[0][0] + strain[1][1] + strain[2][2])
        twice = 2.0 * lame_ref[1, rows, :]
        second = [
            [(trace if a == c else 0.0) + twice * strain[a][c] for c in range(3)] for a in range(3)
        ]
        scaled = [[None] * 3 for _ in range(3)]
        for a in range(3):
            for c in range(3):
                v = sum(deform[a][k] * second[k][c] for k in range(3)) * inside
                piola_ref[3 * a + c, rows, :] = v
                scaled[a][c] = weight * v
        for a in range(3):
            own = sum(scaled[a][c] * column[c] for c in range(3))
            force_ref[a, rows, :] = own + contact_ref[a, rows, :]
            feats = scaled[a] + [sum(scaled[a][c] * here[c] for c in range(3))]
            for f, v in enumerate(feats):
                h, l = parts(v, 2)
                gs[pl.ds(f * 8 + a, GROUP, stride=32), :] = h
                gs[pl.ds(f * 8 + 4 + a, GROUP, stride=32), :] = l

        def backward(q, _):
            b = start + q
            feat = gs[pl.ds(pl.multiple_of(q * 32, 32), 32), :].astype(BF16)
            feat = jnp.concatenate([feat, feat], axis=1)
            for k in range(0, fanout, 2):
                sums = mm(feat, k_all[q, :, pl.ds(k * lanes, 2 * lanes)], NN)
                for j in range(2):
                    t = far[b, k + j]
                    back = [sums[8 * f : 8 * f + 8, j * lanes : (j + 1) * lanes] for f in range(4)]
                    v = back[3] - sum(t[c : c + 1] * back[c] for c in range(3))
                    v = (-coeff * t[6:7]) * v
                    first = start_ref[1, (k + j) * blocks + b]
                    back_ref[pl.ds(first, 3, stride=cap), :] = v[0:3] + v[4:7]
            return 0

        lax.fori_loop(0, GROUP, backward, 0, unroll=4)
        return 0

    lax.fori_loop(0, blocks // GROUP, group, 0)


def returned_kernel(code_ref, got_ref, force_ref, out_ref):
    comps, blocks, lanes = force_ref.shape
    rows = got_ref.shape[0]
    target = lax.broadcasted_iota(jnp.int32, (comps * blocks, rows), 0)
    chosen = (target == code_ref[...]).astype(F32).astype(BF16)
    out = force_ref[...].reshape(comps * blocks, lanes)
    for part in parts(got_ref[...], 2):
        out = out + mm(chosen, part.astype(BF16), NN)
    out_ref[...] = out.reshape(comps, blocks, lanes)


def vmem(count):
    return [pl.BlockSpec(memory_space=pltpu.VMEM)] * count


SMEM = pl.BlockSpec(memory_space=pltpu.SMEM)


def call(body, name, out, in_specs, scratch=(), mib=8, flops=1_000_000, size=1_000_000):
    many = isinstance(out, tuple)
    return pl.pallas_call(
        body,
        out_shape=out,
        in_specs=in_specs,
        out_specs=tuple(vmem(len(out))) if many else vmem(1)[0],
        scratch_shapes=list(scratch),
        compiler_params=pltpu.CompilerParams(vmem_limit_bytes=mib * 2**20),
        cost_estimate=pl.CostEstimate(flops=flops, bytes_accessed=size, transcendentals=0),
        name=name,
    )


def main_call(start, pos_t, disp_t, weight, lame_t, contact, at, centre, got):
    blocks, lanes = weight.shape
    fanout = start.shape[1] // blocks
    wide = fanout * lanes
    back = got.shape[0] // ROWS * 3
    return call(
        main_kernel,
        "pairs",
        (
            jax.ShapeDtypeStruct((9, blocks, lanes), F32),
            jax.ShapeDtypeStruct((3, blocks, lanes), F32),
            jax.ShapeDtypeStruct((back, lanes), F32),
        ),
        [SMEM] + vmem(8),
        [
            pltpu.VMEM((fanout, 8, lanes), F32),
            pltpu.VMEM((blocks, fanout, 8, lanes), F32),
            pltpu.VMEM((blocks, SIDE, wide), BF16),
            pltpu.VMEM((blocks, 64, wide), BF16),
            pltpu.VMEM((GROUP, 2 * lanes, wide), BF16),
            pltpu.VMEM((GROUP * 32, lanes), F32),
            pltpu.VMEM((GROUP * 32, lanes), F32),
        ],
        mib=28,
        flops=60_000_000,
        size=4_000_000,
    )(start, pos_t, disp_t, weight, lame_t, contact, at, centre, got)


def per_device(ref_pos, disp, volume, lame, pad_count, nbr_owner, nbr_local, contact_block):
    blocks, _, lanes = ref_pos.shape
    fanout = nbr_local.shape[1]
    across = lax.axis_size("gx")
    deep = lax.axis_size("yz")
    devices = across * deep
    cap = 2 * blocks * fanout // devices
    total = blocks * fanout
    shape = jax.ShapeDtypeStruct

    ask, start = call(
        lambda *refs: plan_kernel(*refs, cap=cap),
        "plan",
        (shape((devices, 16), jnp.int32), shape((2, total), jnp.int32)),
        vmem(2),
        [pltpu.VMEM((8, total), jnp.int32)],
    )(jnp.transpose(nbr_owner, (1, 2, 0)), jnp.transpose(nbr_local))
    asked = lax.all_to_all(ask, AXES, split_axis=0, concat_axis=0, tiled=True)

    usable = (jnp.arange(lanes)[None, :] < (lanes - pad_count)[:, None]).astype(F32)
    weight = volume * usable
    pos_t = jnp.transpose(ref_pos, (1, 0, 2))
    disp_t = jnp.transpose(disp, (1, 0, 2))
    lame_t = jnp.transpose(lame, (1, 0, 2))

    surface = jnp.concatenate([ref_pos + disp, weight[:, None, :]], axis=1)
    up = [(i, i + 1) for i in range(across - 1)]
    down = [(i + 1, i) for i in range(across - 1)]
    below = lax.ppermute(surface[blocks - SH :], "gx", up)
    above = lax.ppermute(surface[:SH], "gx", down)
    local = contact_block % blocks
    row = contact_block // blocks // deep
    pick = jnp.where(row < lax.axis_index("gx"), local - (blocks - SH), SH + local)

    at, centre = call(
        own_kernel,
        "own",
        (shape((blocks, lanes, SIDE), BF16), shape((blocks * 8, lanes), F32)),
        vmem(1),
        [pltpu.VMEM((GROUP * SIDE, lanes), F32)],
    )(pos_t)

    picked = call(
        lambda *refs: provide_kernel(*refs, cap=cap),
        "provide",
        shape((devices * cap * ROWS, lanes), F32),
        vmem(4),
        [pltpu.VMEM((devices * cap, lanes), jnp.int32)],
    )(asked, pos_t, disp_t, weight)
    got = lax.all_to_all(
        picked.reshape(devices, ROWS, cap, lanes), AXES, split_axis=0, concat_axis=0, tiled=True
    ).reshape(devices * cap * ROWS, lanes)

    contact = call(
        contact_kernel,
        "contact",
        shape((3, blocks, lanes), F32),
        vmem(5) + [SMEM],
        [pltpu.VMEM((2 * SH, 4, lanes, lanes), F32), pltpu.VMEM((3, blocks, lanes), F32)],
        flops=20_000_000,
    )(pos_t, disp_t, weight, below, above, pick)

    piola, force, back = main_call(
        start, pos_t, disp_t, weight, lame_t, contact, at, centre, got
    )
    received = lax.all_to_all(
        back.reshape(devices, 3, cap, lanes), AXES, split_axis=0, concat_axis=0, tiled=True
    )
    ids = asked[:, None, 0:cap]
    code = jnp.where(ids >= 0, ids + blocks * jnp.arange(3)[None, :, None], -1).reshape(1, -1)
    force = call(returned_kernel, "returned", shape((3, blocks, lanes), F32), vmem(3))(
        code, received.reshape(devices * cap * 3, lanes), force
    )
    return (jnp.transpose(force, (1, 0, 2)), jnp.transpose(piola, (1, 0, 2)))


def solution(mesh):
    return jax.shard_map(
        per_device,
        mesh=mesh,
        in_specs=(
            P(AXES, None, None),
            P(AXES, None, None),
            P(AXES, None),
            P(AXES, None, None),
            P(AXES),
            P(AXES, None, None),
            P(AXES, None),
            P(AXES, None),
        ),
        out_specs=(P(AXES, None, None), P(AXES, None, None)),
        check_vma=False,
    )
```

```python
import math

import jax
import jax.numpy as jnp
from jax import lax
from jax.experimental import pallas as pl
from jax.experimental.pallas import tpu as pltpu
from jax.sharding import PartitionSpec as P

SH = 4
SUPPORT_SQ = 0.5
CONTACT_SQ = 0.1
PENALTY = 200.0
GROUP = 8
ROWS = 7
SIDE = 48
F32 = jnp.float32
BF16 = jnp.bfloat16
AXES = ("gx", "yz")
NT = (((1,), (1,)), ((), ()))
NN = (((1,), (0,)), ((), ()))


def high(x):
    return x.astype(BF16).astype(F32)


def parts(x, count):
    out = []
    for _ in range(count - 1):
        h = high(x)
        out.append(h)
        x = x - h
    out.append(high(x))
    return out


def mm(a, b, dims):
    return lax.dot_general(a, b, dims, preferred_element_type=F32)


def plan_kernel(owner_hbm, local_hbm, ask_ref, start_ref, owner_ref, local_ref, rows, sem, *, cap):
    copies = [
        pltpu.make_async_copy(owner_hbm, owner_ref, sem.at[0]),
        pltpu.make_async_copy(local_hbm, local_ref, sem.at[1]),
    ]
    for c in copies:
        c.start()
    fanout, blocks = local_ref.shape
    devices, width = ask_ref.shape
    total = fanout * blocks
    for c in copies:
        c.wait()
    for k in range(fanout):
        cols = pl.ds(k * blocks, blocks)
        rows[0:1, cols] = owner_ref[k]
        rows[1:2, cols] = local_ref[k : k + 1, :]
    owner = rows[0:1, :]
    local = (rows[1:2, :] + 1).astype(F32)
    named = owner == lax.broadcasted_iota(jnp.int32, (devices, total), 0)
    hot = named.astype(F32)
    earlier = lax.broadcasted_iota(jnp.int32, (total, total), 0) < lax.broadcasted_iota(
        jnp.int32, (total, total), 1
    )
    rank = mm(hot.astype(BF16), earlier.astype(F32).astype(BF16), NN)
    lane = lax.broadcasted_iota(jnp.int32, (width, total), 0)
    ask = jnp.zeros((devices, width), F32)
    for s in range(cap):
        chosen = jnp.where(rank == float(s), hot, 0.0).astype(BF16)
        ask = ask + mm(chosen, jnp.where(lane == s, local, 0.0).astype(BF16), NT)
    ask_ref[...] = ask.astype(jnp.int32) - 1
    place = jnp.sum(hot * rank, axis=0, keepdims=True).astype(jnp.int32)
    start_ref[0:1, :] = owner * (cap * ROWS) + place
    start_ref[1:2, :] = owner * (cap * 3) + place


def provide_kernel(ask_ref, data_ref, out_hbm, wide, out, sem, *, cap):
    devices = ask_ref.shape[0]
    depth = data_ref.shape[0]
    lanes = data_ref.shape[1] // ROWS
    blocks = depth // 3
    for s in range(cap):
        wide[pl.ds(s, devices, stride=cap), :] = jnp.broadcast_to(
            ask_ref[:, s : s + 1], (devices, lanes)
        )
    step = 64
    local = lax.broadcasted_iota(jnp.int32, (step, depth), 1) % blocks
    copies = []
    for i in range(devices * cap // step):
        hot = (wide[pl.ds(i * step, step), 0:depth] == local).astype(F32).astype(BF16)
        got = mm(hot, data_ref[...], NN)
        for j in range(step // cap):
            r = i * (step // cap) + j
            for c in range(ROWS):
                out[pl.ds((r * ROWS + c) * cap, cap), :] = got[
                    j * cap : (j + 1) * cap, c * lanes : (c + 1) * lanes
                ]
        if i % 2:
            rows = pl.ds((i - 1) * step * ROWS, 2 * step * ROWS)
            copies.append(pltpu.make_async_copy(out.at[rows], out_hbm.at[rows], sem.at[i // 2]))
            copies[-1].start()
    for c in copies:
        c.wait()


def own_kernel(pos_ref, disp_ref, weight_ref, at_ref, centre_ref, data_ref, side):
    _, blocks, lanes = pos_ref.shape
    inv = 1.0 / SUPPORT_SQ
    for c in range(ROWS):
        x = weight_ref[...] if c == 6 else (pos_ref if c < 3 else disp_ref)[c % 3]
        data_ref[:, c * lanes : (c + 1) * lanes] = jnp.concatenate(parts(x, 3), axis=0).astype(BF16)
    side[...] = jnp.zeros_like(side)
    centre_ref[...] = jnp.zeros_like(centre_ref)
    ones = jnp.ones((GROUP, lanes), F32)
    for d in (0, 3, 5):
        side[pl.ds(d * 8 + 7, GROUP, stride=SIDE), :] = ones

    def group(g, _):
        start = pl.multiple_of(g * GROUP, GROUP)
        norm = jnp.zeros((GROUP, lanes), F32)
        for c in range(3):
            x = pos_ref[c, pl.ds(start, GROUP), :]
            mid = jnp.broadcast_to(x[:, 0:1], x.shape)
            x = x - mid
            centre_ref[pl.ds(start * 8 + c, GROUP, stride=8), :] = mid
            norm = norm + x * x
            h, m, l = [2.0 * inv * p for p in parts(x, 3)]
            for d, v in enumerate((h, m, l, h, m, h)):
                side[pl.ds(d * 8 + c, GROUP, stride=SIDE), :] = v
        for d, v in enumerate(parts(1.0 - inv * norm, 3)):
            side[pl.ds(d * 8 + 3, GROUP, stride=SIDE), :] = v
        for q in range(GROUP):
            at_ref[start + q] = jnp.transpose(side[pl.ds(q * SIDE, SIDE), :]).astype(BF16)
        return 0

    lax.fori_loop(0, blocks // GROUP, group, 0)


def contact_kernel(
    pos_ref, disp_ref, weight_ref, below_ref, above_ref, pick_ref, force_ref, out_ref, wide, cur
):
    blocks, lanes = weight_ref.shape
    half = below_ref.shape[0]
    for c in range(3):
        cur[c] = pos_ref[c] + disp_ref[c]
    for s in range(2 * half):
        block = below_ref[s] if s < half else above_ref[s - half]
        turned = jnp.transpose(jnp.concatenate([block, block], axis=0))
        for c in range(4):
            wide[s, c] = jnp.broadcast_to(turned[:, c : c + 1], (lanes, lanes))

    def block(b, _):
        own = [jnp.broadcast_to(cur[c, pl.ds(b, 1), :], (8, lanes)) for c in range(3)]
        total = [jnp.zeros((8, lanes), F32) for _ in range(3)]
        for k in range(2):
            s = pick_ref[b, k]
            for r in range(lanes // 8):
                rows = pl.ds(r * 8, 8)
                gap = [own[c] - wide[s, c, rows, :] for c in range(3)]
                near = jnp.maximum(
                    CONTACT_SQ - (gap[0] * gap[0] + gap[1] * gap[1] + gap[2] * gap[2]), 0.0
                )
                push = near * near * wide[s, 3, rows, :]
                total = [total[c] + push * gap[c] for c in range(3)]
        scale = PENALTY * (weight_ref[pl.ds(b, 1), :] > 0).astype(F32)
        for c in range(3):
            push = scale * jnp.sum(total[c], axis=0, keepdims=True)
            out_ref[c, pl.ds(b, 1), :] = force_ref[c, pl.ds(b, 1), :] + push
        return 0

    lax.fori_loop(0, blocks, block, 0)


def main_kernel(
    start_ref, pos_ref, disp_ref, weight_ref, lame_ref, at_ref, centre_ref, got_ref,
    piola_ref, force_ref, back_hbm,
    raw, far, b_all, f_all, k_all, ss, gs, back_ref, sem,
):
    blocks, lanes = weight_ref.shape
    fanout = far.shape[1]
    cap = 4
    coeff = -3.0 / math.sqrt(fanout * lanes)
    inv = 1.0 / SUPPORT_SQ
    back_ref[...] = jnp.zeros_like(back_ref)
    gs[...] = jnp.zeros_like(gs)
    raw[...] = jnp.zeros_like(raw)
    row = lax.broadcasted_iota(jnp.int32, (8, lanes), 0)

    def far_side(b, _):
        centre = centre_ref[pl.ds(pl.multiple_of(b * 8, 8), 8), :]
        for k in range(fanout):
            raw[k, 0:ROWS, :] = got_ref[pl.ds(start_ref[0, k * blocks + b], ROWS, stride=cap), :]
        for k in range(fanout):
            t = raw[k] - centre
            far[b, k] = t
            square = t * t
            norm = square[0:1] + square[1:2] + square[2:3]
            place = jnp.where(row == 3, 1.0, jnp.where(row == 7, -inv * norm, t))
            h, m, l = parts(place, 3)
            cols = pl.ds(k * lanes, lanes)
            b_all[b, :, cols] = jnp.concatenate([h, h, h, m, m, l], axis=0).astype(BF16)
            weight = t[6:7]
            plain = jnp.where(row == 6, 1.0, t)
            feats = [weight * plain] + [(weight * t[3 + a : 4 + a]) * plain for a in range(3)]
            split = [parts(v, 2) for v in feats]
            f_all[b, :, cols] = jnp.concatenate(
                [v[0] for v in split] + [v[1] for v in split], axis=0
            ).astype(BF16)
        return 0


    def group(g, _):
        start = pl.multiple_of(g * GROUP, GROUP)
        rows = pl.ds(start, GROUP)

        def forward(q, _):
            b = start + q
            far_side(b, 0)
            sums = jnp.zeros((64, 2 * lanes), F32)
            for k in range(0, fanout, 8):
                cols = pl.ds(k * lanes, 8 * lanes)
                near = jnp.maximum(mm(at_ref[b], b_all[b, :, cols], NN), 0.0)
                near = near * near
                hi = near.astype(BF16)
                lo = (near - hi.astype(F32)).astype(BF16)
                both = jnp.concatenate([hi, lo], axis=0)
                k_all[q, :, cols] = both
                sums = sums + mm(f_all[b, :, cols], both, NT)
            sums = sums[:, 0:lanes] + sums[:, lanes:]
            ss[pl.ds(pl.multiple_of(q * 32, 32), 32), :] = sums[0:32] + sums[32:64]
            return 0

        lax.fori_loop(0, GROUP, forward, 0, unroll=8)

        def total(f):
            return ss[pl.ds(f, GROUP, stride=32), :]

        mass = total(6)
        weight = weight_ref[rows, :]
        inside = (weight > 0).astype(F32)
        here = [pos_ref[c, rows, :] for c in range(3)]
        here = [x - x[:, 0:1] for x in here]
        moved = [disp_ref[c, rows, :] for c in range(3)]
        column = [coeff * (here[c] * mass - total(c)) for c in range(3)]
        deform = [
            [
                (1.0 if a == c else 0.0)
                + coeff * (here[c] * total(3 + a) - total(8 + 8 * a + c))
                - moved[a] * column[c]
                for c in range(3)
            ]
            for a in range(3)
        ]
        strain = [[None] * 3 for _ in range(3)]
        for a in range(3):
            for c in range(a, 3):
                v = sum(deform[k][a] * deform[k][c] for k in range(3))
                strain[a][c] = strain[c][a] = 0.5 * (v - (1.0 if a == c else 0.0))
        trace = lame_ref[0, rows, :] * (strain[0][0] + strain[1][1] + strain[2][2])
        twice = 2.0 * lame_ref[1, rows, :]
        second = [
            [(trace if a == c else 0.0) + twice * strain[a][c] for c in range(3)] for a in range(3)
        ]
        scaled = [[None] * 3 for _ in range(3)]
        for a in range(3):
            for c in range(3):
                v = sum(deform[a][k] * second[k][c] for k in range(3)) * inside
                piola_ref[3 * a + c, rows, :] = v
                scaled[a][c] = weight * v
        for a in range(3):
            own = sum(scaled[a][c] * column[c] for c in range(3))
            force_ref[a, rows, :] = own
            feats = scaled[a] + [sum(scaled[a][c] * here[c] for c in range(3))]
            for f, v in enumerate(feats):
                h, l = parts(v, 2)
                gs[pl.ds(f * 8 + a, GROUP, stride=32), :] = h
                gs[pl.ds(f * 8 + 4 + a, GROUP, stride=32), :] = l

        def backward(q, _):
            b = start + q
            feat = gs[pl.ds(pl.multiple_of(q * 32, 32), 32), :].astype(BF16)
            feat = jnp.concatenate([feat, feat], axis=1)
            for k in range(0, fanout, 2):
                sums = mm(feat, k_all[q, :, pl.ds(k * lanes, 2 * lanes)], NN)
                for j in range(2):
                    t = far[b, k + j]
                    back = [sums[8 * f : 8 * f + 8, j * lanes : (j + 1) * lanes] for f in range(4)]
                    v = back[3] - sum(t[c : c + 1] * back[c] for c in range(3))
                    v = (-coeff * t[6:7]) * v
                    first = start_ref[1, (k + j) * blocks + b]
                    back_ref[pl.ds(first, 3, stride=cap), :] = v[0:3] + v[4:7]
            return 0

        lax.fori_loop(0, GROUP, backward, 0, unroll=8)
        return 0

    lax.fori_loop(0, blocks // GROUP, group, 0)
    copy = pltpu.make_async_copy(back_ref, back_hbm, sem)
    copy.start()
    copy.wait()


def returned_kernel(code_ref, got_ref, force_ref, out_ref):
    comps, blocks, lanes = force_ref.shape
    rows = got_ref.shape[0]
    target = lax.broadcasted_iota(jnp.int32, (comps * blocks, rows), 0)
    chosen = (target == code_ref[...]).astype(F32).astype(BF16)
    out = force_ref[...].reshape(comps * blocks, lanes)
    for part in parts(got_ref[...], 2):
        out = out + mm(chosen, part.astype(BF16), NN)
    out_ref[...] = out.reshape(comps, blocks, lanes)


def vmem(count):
    return [pl.BlockSpec(memory_space=pltpu.VMEM)] * count


SMEM = pl.BlockSpec(memory_space=pltpu.SMEM)
ANY = pl.BlockSpec(memory_space=pl.ANY)


def call(body, name, out, in_specs, scratch=(), kib=8192, flops=1_000_000, size=1_000_000, out_any=False):
    many = isinstance(out, tuple)
    return pl.pallas_call(
        body,
        out_shape=out,
        in_specs=in_specs,
        out_specs=(tuple(vmem(len(out) - out_any) + [ANY] * out_any) if many else ANY if out_any else vmem(1)[0]),
        scratch_shapes=list(scratch),
        compiler_params=pltpu.CompilerParams(vmem_limit_bytes=kib * 2**10),
        cost_estimate=pl.CostEstimate(flops=flops, bytes_accessed=size, transcendentals=0),
        name=name,
    )


def main_call(start, pos_t, disp_t, weight, lame_t, at, centre, got):
    blocks, lanes = weight.shape
    fanout = start.shape[1] // blocks
    wide = fanout * lanes
    back = got.shape[0] // ROWS * 3
    return call(
        main_kernel,
        "pairs",
        (
            jax.ShapeDtypeStruct((9, blocks, lanes), F32),
            jax.ShapeDtypeStruct((3, blocks, lanes), F32),
            jax.ShapeDtypeStruct((back, lanes), F32),
        ),
        [SMEM] + vmem(7),
        [
            pltpu.VMEM((fanout, 8, lanes), F32),
            pltpu.VMEM((blocks, fanout, 8, lanes), F32),
            pltpu.VMEM((blocks, SIDE, wide), BF16),
            pltpu.VMEM((blocks, 64, wide), BF16),
            pltpu.VMEM((GROUP, 2 * lanes, wide), BF16),
            pltpu.VMEM((GROUP * 32, lanes), F32),
            pltpu.VMEM((GROUP * 32, lanes), F32),
            pltpu.VMEM((back, lanes), F32),
            pltpu.SemaphoreType.DMA,
        ],
        out_any=True,
        kib=28672,
        flops=60_000_000,
        size=4_000_000,
    )(start, pos_t, disp_t, weight, lame_t, at, centre, got)


def per_device(ref_pos, disp, volume, lame, pad_count, nbr_owner, nbr_local, contact_block):
    blocks, _, lanes = ref_pos.shape
    fanout = nbr_local.shape[1]
    across = lax.axis_size("gx")
    deep = lax.axis_size("yz")
    devices = across * deep
    cap = 2 * blocks * fanout // devices
    total = blocks * fanout
    shape = jax.ShapeDtypeStruct

    ask, start = call(
        lambda *refs: plan_kernel(*refs, cap=cap),
        "plan",
        (shape((devices, 16), jnp.int32), shape((2, total), jnp.int32)),
        [ANY] * 2,
        [
            pltpu.VMEM((fanout, 1, blocks), jnp.int32),
            pltpu.VMEM((fanout, blocks), jnp.int32),
            pltpu.VMEM((8, total), jnp.int32),
            pltpu.SemaphoreType.DMA((2,)),
        ],
        kib=65472,
    )(jnp.transpose(nbr_owner, (1, 2, 0)), jnp.transpose(nbr_local))
    asked = lax.all_to_all(ask, AXES, split_axis=0, concat_axis=0, tiled=True)

    usable = (jnp.arange(lanes)[None, :] < (lanes - pad_count)[:, None]).astype(F32)
    weight = volume * usable
    pos_t = jnp.transpose(ref_pos, (1, 0, 2))
    disp_t = jnp.transpose(disp, (1, 0, 2))
    lame_t = jnp.transpose(lame, (1, 0, 2))

    surface = jnp.concatenate([ref_pos + disp, weight[:, None, :]], axis=1)
    up = [(i, i + 1) for i in range(across - 1)]
    down = [(i + 1, i) for i in range(across - 1)]
    below = lax.ppermute(surface[blocks - SH :], "gx", up)
    above = lax.ppermute(surface[:SH], "gx", down)
    local = contact_block % blocks
    row = contact_block // blocks // deep
    pick = jnp.where(row < lax.axis_index("gx"), local - (blocks - SH), SH + local)

    at, centre, data = call(
        own_kernel,
        "own",
        (
            shape((blocks, lanes, SIDE), BF16),
            shape((blocks * 8, lanes), F32),
            shape((3 * blocks, ROWS * lanes), BF16),
        ),
        vmem(3),
        [pltpu.VMEM((GROUP * SIDE, lanes), F32)],
    )(pos_t, disp_t, weight)

    picked = call(
        lambda *refs: provide_kernel(*refs, cap=cap),
        "provide",
        shape((devices * cap * ROWS, lanes), F32),
        vmem(2),
        [
            pltpu.VMEM((devices * cap, lanes), jnp.int32),
            pltpu.VMEM((devices * cap * ROWS, lanes), F32),
            pltpu.SemaphoreType.DMA((devices * cap // 128,)),
        ],
        out_any=True,
        kib=64000,
    )(asked, data)
    got = lax.all_to_all(
        picked.reshape(devices, ROWS, cap, lanes), AXES, split_axis=0, concat_axis=0, tiled=True
    ).reshape(devices * cap * ROWS, lanes)

    piola, force, back = main_call(start, pos_t, disp_t, weight, lame_t, at, centre, got)
    received = lax.all_to_all(
        back.reshape(devices, 3, cap, lanes), AXES, split_axis=0, concat_axis=0, tiled=True
    )
    force = call(
        contact_kernel,
        "contact",
        shape((3, blocks, lanes), F32),
        vmem(5) + [SMEM] + vmem(1),
        [pltpu.VMEM((2 * SH, 4, lanes, lanes), F32), pltpu.VMEM((3, blocks, lanes), F32)],
        flops=20_000_000,
    )(pos_t, disp_t, weight, below, above, pick, force)
    ids = asked[:, None, 0:cap]
    code = jnp.where(ids >= 0, ids + blocks * jnp.arange(3)[None, :, None], -1).reshape(1, -1)
    force = call(returned_kernel, "returned", shape((3, blocks, lanes), F32), vmem(3))(
        code, received.reshape(devices * cap * 3, lanes), force
    )
    return (jnp.transpose(force, (1, 0, 2)), jnp.transpose(piola, (1, 0, 2)))


def solution(mesh):
    return jax.shard_map(
        per_device,
        mesh=mesh,
        in_specs=(
            P(AXES, None, None),
            P(AXES, None, None),
            P(AXES, None),
            P(AXES, None, None),
            P(AXES),
            P(AXES, None, None),
            P(AXES, None),
            P(AXES, None),
        ),
        out_specs=(P(AXES, None, None), P(AXES, None, None)),
        check_vma=False,
    )
```

```python
import math

import jax
import jax.numpy as jnp
from jax import lax
from jax.experimental import pallas as pl
from jax.experimental.pallas import tpu as pltpu
from jax.sharding import PartitionSpec as P

SH = 4
SUPPORT_SQ = 0.5
CONTACT_SQ = 0.1
PENALTY = 200.0
GROUP = 8
ROWS = 7
SIDE = 48
F32 = jnp.float32
BF16 = jnp.bfloat16
AXES = ("gx", "yz")
NT = (((1,), (1,)), ((), ()))
NN = (((1,), (0,)), ((), ()))


def high(x):
    return x.astype(BF16).astype(F32)


def parts(x, count):
    out = []
    for _ in range(count - 1):
        h = high(x)
        out.append(h)
        x = x - h
    out.append(high(x))
    return out


def mm(a, b, dims):
    return lax.dot_general(a, b, dims, preferred_element_type=F32)


def plan_kernel(owner_hbm, local_hbm, ask_ref, start_ref, owner_ref, local_ref, rows, sem, *, cap):
    copies = [
        pltpu.make_async_copy(owner_hbm, owner_ref, sem.at[0]),
        pltpu.make_async_copy(local_hbm, local_ref, sem.at[1]),
    ]
    for c in copies:
        c.start()
    fanout, blocks = local_ref.shape
    devices, width = ask_ref.shape
    total = fanout * blocks
    earlier = lax.broadcasted_iota(jnp.int32, (total, total), 0) < lax.broadcasted_iota(
        jnp.int32, (total, total), 1
    )
    earlier = earlier.astype(F32).astype(BF16)
    for c in copies:
        c.wait()
    for k in range(fanout):
        cols = pl.ds(k * blocks, blocks)
        rows[0:1, cols] = owner_ref[k]
        rows[1:2, cols] = local_ref[k : k + 1, :]
    owner = rows[0:1, :]
    local = (rows[1:2, :] + 1).astype(F32)
    named = owner == lax.broadcasted_iota(jnp.int32, (devices, total), 0)
    hot = named.astype(F32)
    rank = mm(hot.astype(BF16), earlier, NN)
    lane = lax.broadcasted_iota(jnp.int32, (width, total), 0)
    ask = jnp.zeros((devices, width), F32)
    for s in range(cap):
        chosen = jnp.where(rank == float(s), hot, 0.0).astype(BF16)
        ask = ask + mm(chosen, jnp.where(lane == s, local, 0.0).astype(BF16), NT)
    ask_ref[...] = ask.astype(jnp.int32) - 1
    place = jnp.sum(hot * rank, axis=0, keepdims=True).astype(jnp.int32)
    start_ref[0:1, :] = owner * (cap * ROWS) + place
    start_ref[1:2, :] = owner * (cap * 3) + place


def provide_kernel(ask_ref, data_ref, out, wide, *, cap):
    devices = ask_ref.shape[0]
    depth = data_ref.shape[0]
    lanes = data_ref.shape[1] // ROWS
    blocks = depth // 3
    for s in range(cap):
        wide[pl.ds(s, devices, stride=cap), :] = jnp.broadcast_to(
            ask_ref[:, s : s + 1], (devices, lanes)
        )
    step = 64
    local = lax.broadcasted_iota(jnp.int32, (step, depth), 1) % blocks
    for i in range(devices * cap // step):
        hot = (wide[pl.ds(i * step, step), 0:depth] == local).astype(F32).astype(BF16)
        got = mm(hot, data_ref[...], NN)
        for j in range(step // cap):
            r = i * (step // cap) + j
            for c in range(ROWS):
                out[pl.ds((r * ROWS + c) * cap, cap), :] = got[
                    j * cap : (j + 1) * cap, c * lanes : (c + 1) * lanes
                ]


def own_kernel(pos_ref, disp_ref, weight_ref, at_ref, centre_ref, data_ref, side):
    _, blocks, lanes = pos_ref.shape
    inv = 1.0 / SUPPORT_SQ
    for c in range(ROWS):
        x = weight_ref[...] if c == 6 else (pos_ref if c < 3 else disp_ref)[c % 3]
        data_ref[:, c * lanes : (c + 1) * lanes] = jnp.concatenate(parts(x, 3), axis=0).astype(BF16)
    side[...] = jnp.zeros_like(side)
    centre_ref[...] = jnp.zeros_like(centre_ref)
    ones = jnp.ones((GROUP, lanes), F32)
    for d in (0, 3, 5):
        side[pl.ds(d * 8 + 7, GROUP, stride=SIDE), :] = ones

    def group(g, _):
        start = pl.multiple_of(g * GROUP, GROUP)
        norm = jnp.zeros((GROUP, lanes), F32)
        for c in range(3):
            x = pos_ref[c, pl.ds(start, GROUP), :]
            mid = jnp.broadcast_to(x[:, 0:1], x.shape)
            x = x - mid
            centre_ref[pl.ds(start * 8 + c, GROUP, stride=8), :] = mid
            norm = norm + x * x
            h, m, l = [2.0 * inv * p for p in parts(x, 3)]
            for d, v in enumerate((h, m, l, h, m, h)):
                side[pl.ds(d * 8 + c, GROUP, stride=SIDE), :] = v
        for d, v in enumerate(parts(1.0 - inv * norm, 3)):
            side[pl.ds(d * 8 + 3, GROUP, stride=SIDE), :] = v
        for q in range(GROUP):
            at_ref[start + q] = jnp.transpose(side[pl.ds(q * SIDE, SIDE), :]).astype(BF16)
        return 0

    lax.fori_loop(0, blocks // GROUP, group, 0)


def contact_kernel(
    pos_ref, disp_ref, weight_ref, below_ref, above_ref, pick_ref, force_ref, out_ref, wide, cur
):
    blocks, lanes = weight_ref.shape
    half = below_ref.shape[0]
    for c in range(3):
        cur[c] = pos_ref[c] + disp_ref[c]
    for s in range(2 * half):
        block = below_ref[s] if s < half else above_ref[s - half]
        turned = jnp.transpose(jnp.concatenate([block, block], axis=0))
        for c in range(4):
            wide[s, c] = jnp.broadcast_to(turned[:, c : c + 1], (lanes, lanes))

    def block(b, _):
        own = [jnp.broadcast_to(cur[c, pl.ds(b, 1), :], (8, lanes)) for c in range(3)]
        total = [jnp.zeros((8, lanes), F32) for _ in range(3)]
        for k in range(2):
            s = pick_ref[b, k]
            for r in range(lanes // 8):
                rows = pl.ds(r * 8, 8)
                gap = [own[c] - wide[s, c, rows, :] for c in range(3)]
                near = jnp.maximum(
                    CONTACT_SQ - (gap[0] * gap[0] + gap[1] * gap[1] + gap[2] * gap[2]), 0.0
                )
                push = near * near * wide[s, 3, rows, :]
                total = [total[c] + push * gap[c] for c in range(3)]
        scale = PENALTY * (weight_ref[pl.ds(b, 1), :] > 0).astype(F32)
        for c in range(3):
            push = scale * jnp.sum(total[c], axis=0, keepdims=True)
            out_ref[c, pl.ds(b, 1), :] = force_ref[c, pl.ds(b, 1), :] + push
        return 0

    lax.fori_loop(0, blocks, block, 0)


def main_kernel(
    start_ref, pos_ref, disp_ref, weight_ref, lame_ref, at_ref, centre_ref, got_ref,
    piola_ref, force_ref, back_ref,
    raw, far, b_all, f_all, k_all, ss, gs,
):
    blocks, lanes = weight_ref.shape
    fanout = far.shape[1]
    cap = 4
    coeff = -3.0 / math.sqrt(fanout * lanes)
    inv = 1.0 / SUPPORT_SQ
    back_ref[...] = jnp.zeros_like(back_ref)
    gs[...] = jnp.zeros_like(gs)
    raw[...] = jnp.zeros_like(raw)
    row = lax.broadcasted_iota(jnp.int32, (8, lanes), 0)

    def far_side(b, _):
        centre = centre_ref[pl.ds(pl.multiple_of(b * 8, 8), 8), :]
        for k in range(fanout):
            raw[k, 0:ROWS, :] = got_ref[pl.ds(start_ref[0, k * blocks + b], ROWS, stride=cap), :]
        for k in range(fanout):
            t = raw[k] - centre
            far[b, k] = t
            square = t * t
            norm = square[0:1] + square[1:2] + square[2:3]
            place = jnp.where(row == 3, 1.0, jnp.where(row == 7, -inv * norm, t))
            h, m, l = parts(place, 3)
            cols = pl.ds(k * lanes, lanes)
            b_all[b, :, cols] = jnp.concatenate([h, h, h, m, m, l], axis=0).astype(BF16)
            weight = t[6:7]
            plain = jnp.where(row == 6, 1.0, t)
            feats = [weight * plain] + [(weight * t[3 + a : 4 + a]) * plain for a in range(3)]
            split = [parts(v, 2) for v in feats]
            f_all[b, :, cols] = jnp.concatenate(
                [v[0] for v in split] + [v[1] for v in split], axis=0
            ).astype(BF16)
        return 0


    def group(g, _):
        start = pl.multiple_of(g * GROUP, GROUP)
        rows = pl.ds(start, GROUP)
        turn = g % 2

        def forward(q, _):
            b = start + q
            far_side(b, 0)
            near = jnp.maximum(mm(at_ref[b], b_all[b], NN), 0.0)
            near = near * near
            hi = near.astype(BF16)
            lo = (near - hi.astype(F32)).astype(BF16)
            k_all[turn * GROUP + q, 0:lanes, :] = hi
            k_all[turn * GROUP + q, lanes:, :] = lo
            feat = f_all[b]
            sums = mm(
                jnp.concatenate([hi, lo], axis=1), jnp.concatenate([feat, feat], axis=1), NT
            )
            sums = jnp.transpose(sums)
            ss[turn, pl.ds(pl.multiple_of(q * 32, 32), 32), :] = sums[0:32] + sums[32:64]
            return 0

        lax.fori_loop(0, GROUP, forward, 0, unroll=8)

        def total(f):
            return ss[turn, pl.ds(f, GROUP, stride=32), :]

        mass = total(6)
        weight = weight_ref[rows, :]
        inside = (weight > 0).astype(F32)
        here = [pos_ref[c, rows, :] for c in range(3)]
        here = [x - x[:, 0:1] for x in here]
        moved = [disp_ref[c, rows, :] for c in range(3)]
        column = [coeff * (here[c] * mass - total(c)) for c in range(3)]
        deform = [
            [
                (1.0 if a == c else 0.0)
                + coeff * (here[c] * total(3 + a) - total(8 + 8 * a + c))
                - moved[a] * column[c]
                for c in range(3)
            ]
            for a in range(3)
        ]
        strain = [[None] * 3 for _ in range(3)]
        for a in range(3):
            for c in range(a, 3):
                v = sum(deform[k][a] * deform[k][c] for k in range(3))
                strain[a][c] = strain[c][a] = 0.5 * (v - (1.0 if a == c else 0.0))
        trace = lame_ref[0, rows, :] * (strain[0][0] + strain[1][1] + strain[2][2])
        twice = 2.0 * lame_ref[1, rows, :]
        second = [
            [(trace if a == c else 0.0) + twice * strain[a][c] for c in range(3)] for a in range(3)
        ]
        scaled = [[None] * 3 for _ in range(3)]
        for a in range(3):
            for c in range(3):
                v = sum(deform[a][k] * second[k][c] for k in range(3)) * inside
                piola_ref[3 * a + c, rows, :] = v
                scaled[a][c] = weight * v
        for a in range(3):
            own = sum(scaled[a][c] * column[c] for c in range(3))
            force_ref[a, rows, :] = own
            feats = scaled[a] + [sum(scaled[a][c] * here[c] for c in range(3))]
            for f, v in enumerate(feats):
                h, l = parts(v, 2)
                gs[turn, pl.ds(f * 8 + a, GROUP, stride=32), :] = h
                gs[turn, pl.ds(f * 8 + 4 + a, GROUP, stride=32), :] = l

        def backward(q, _):
            b = start + q
            feat = gs[turn, pl.ds(pl.multiple_of(q * 32, 32), 32), :].astype(BF16)
            feat = jnp.concatenate([feat, feat], axis=1)
            for k in range(0, fanout, 2):
                sums = mm(feat, k_all[turn * GROUP + q, :, pl.ds(k * lanes, 2 * lanes)], NN)
                for j in range(2):
                    back = [sums[8 * f : 8 * f + 8, j * lanes : (j + 1) * lanes] for f in range(4)]
                    cast = [far[b, k + j, pl.ds(c, 8, stride=0), :] for c in (0, 1, 2, 6)]
                    v = back[3] - sum(cast[c] * back[c] for c in range(3))
                    v = (-coeff * cast[3]) * v
                    first = start_ref[1, (k + j) * blocks + b]
                    back_ref[pl.ds(first, 3, stride=cap), :] = v[0:3] + v[4:7]
            return 0

        lax.fori_loop(0, GROUP, backward, 0, unroll=8)
        return 0

    lax.fori_loop(0, blocks // GROUP, group, 0, unroll=4)


def returned_kernel(code_ref, got_ref, force_ref, out_ref):
    comps, blocks, lanes = force_ref.shape
    rows = got_ref.shape[0]
    target = lax.broadcasted_iota(jnp.int32, (comps * blocks, rows), 0)
    chosen = (target == code_ref[...]).astype(F32).astype(BF16)
    out = force_ref[...].reshape(comps * blocks, lanes)
    for part in parts(got_ref[...], 2):
        out = out + mm(chosen, part.astype(BF16), NN)
    out_ref[...] = out.reshape(comps, blocks, lanes)


def vmem(count):
    return [pl.BlockSpec(memory_space=pltpu.VMEM)] * count


SMEM = pl.BlockSpec(memory_space=pltpu.SMEM)
ANY = pl.BlockSpec(memory_space=pl.ANY)


def call(body, name, out, in_specs, scratch=(), kib=8192, flops=1_000_000, size=1_000_000):
    many = isinstance(out, tuple)
    return pl.pallas_call(
        body,
        out_shape=out,
        in_specs=in_specs,
        out_specs=tuple(vmem(len(out))) if many else vmem(1)[0],
        scratch_shapes=list(scratch),
        compiler_params=pltpu.CompilerParams(vmem_limit_bytes=kib * 2**10),
        cost_estimate=pl.CostEstimate(flops=flops, bytes_accessed=size, transcendentals=0),
        name=name,
    )


def main_call(start, pos_t, disp_t, weight, lame_t, at, centre, got):
    blocks, lanes = weight.shape
    fanout = start.shape[1] // blocks
    wide = fanout * lanes
    back = got.shape[0] // ROWS * 3
    return call(
        main_kernel,
        "pairs",
        (
            jax.ShapeDtypeStruct((9, blocks, lanes), F32),
            jax.ShapeDtypeStruct((3, blocks, lanes), F32),
            jax.ShapeDtypeStruct((back, lanes), F32),
        ),
        [SMEM] + vmem(7),
        [
            pltpu.VMEM((fanout, 8, lanes), F32),
            pltpu.VMEM((blocks, fanout, 8, lanes), F32),
            pltpu.VMEM((blocks, SIDE, wide), BF16),
            pltpu.VMEM((blocks, 64, wide), BF16),
            pltpu.VMEM((2 * GROUP, 2 * lanes, wide), BF16),
            pltpu.VMEM((2, GROUP * 32, lanes), F32),
            pltpu.VMEM((2, GROUP * 32, lanes), F32),
        ],
        kib=36000,
        flops=60_000_000,
        size=4_000_000,
    )(start, pos_t, disp_t, weight, lame_t, at, centre, got)


def per_device(ref_pos, disp, volume, lame, pad_count, nbr_owner, nbr_local, contact_block):
    blocks, _, lanes = ref_pos.shape
    fanout = nbr_local.shape[1]
    across = lax.axis_size("gx")
    deep = lax.axis_size("yz")
    devices = across * deep
    cap = 2 * blocks * fanout // devices
    total = blocks * fanout
    shape = jax.ShapeDtypeStruct

    ask, start = call(
        lambda *refs: plan_kernel(*refs, cap=cap),
        "plan",
        (shape((devices, 16), jnp.int32), shape((2, total), jnp.int32)),
        [ANY] * 2,
        [
            pltpu.VMEM((fanout, 1, blocks), jnp.int32),
            pltpu.VMEM((fanout, blocks), jnp.int32),
            pltpu.VMEM((8, total), jnp.int32),
            pltpu.SemaphoreType.DMA((2,)),
        ],
        kib=65472,
    )(jnp.transpose(nbr_owner, (1, 2, 0)), jnp.transpose(nbr_local))
    asked = lax.all_to_all(ask, AXES, split_axis=0, concat_axis=0, tiled=True)

    usable = (jnp.arange(lanes)[None, :] < (lanes - pad_count)[:, None]).astype(F32)
    weight = volume * usable
    pos_t = jnp.transpose(ref_pos, (1, 0, 2))
    disp_t = jnp.transpose(disp, (1, 0, 2))
    lame_t = jnp.transpose(lame, (1, 0, 2))

    surface = jnp.concatenate([ref_pos + disp, weight[:, None, :]], axis=1)
    up = [(i, i + 1) for i in range(across - 1)]
    down = [(i + 1, i) for i in range(across - 1)]
    below = lax.ppermute(surface[blocks - SH :], "gx", up)
    above = lax.ppermute(surface[:SH], "gx", down)
    local = contact_block % blocks
    row = contact_block // blocks // deep
    pick = jnp.where(row < lax.axis_index("gx"), local - (blocks - SH), SH + local)

    at, centre, data = call(
        own_kernel,
        "own",
        (
            shape((blocks, lanes, SIDE), BF16),
            shape((blocks * 8, lanes), F32),
            shape((3 * blocks, ROWS * lanes), BF16),
        ),
        vmem(3),
        [pltpu.VMEM((GROUP * SIDE, lanes), F32)],
    )(pos_t, disp_t, weight)

    picked = call(
        lambda *refs: provide_kernel(*refs, cap=cap),
        "provide",
        shape((devices * cap * ROWS, lanes), F32),
        vmem(2),
        [pltpu.VMEM((devices * cap, lanes), jnp.int32)],
    )(asked, data)
    got = lax.all_to_all(
        picked.reshape(devices, ROWS, cap, lanes), AXES, split_axis=0, concat_axis=0, tiled=True
    ).reshape(devices * cap * ROWS, lanes)

    piola, force, back = main_call(start, pos_t, disp_t, weight, lame_t, at, centre, got)
    received = lax.all_to_all(
        back.reshape(devices, 3, cap, lanes), AXES, split_axis=0, concat_axis=0, tiled=True
    )
    force = call(
        contact_kernel,
        "contact",
        shape((3, blocks, lanes), F32),
        vmem(5) + [SMEM] + vmem(1),
        [pltpu.VMEM((2 * SH, 4, lanes, lanes), F32), pltpu.VMEM((3, blocks, lanes), F32)],
        flops=20_000_000,
    )(pos_t, disp_t, weight, below, above, pick, force)
    ids = asked[:, None, 0:cap]
    code = jnp.where(ids >= 0, ids + blocks * jnp.arange(3)[None, :, None], -1).reshape(1, -1)
    force = call(returned_kernel, "returned", shape((3, blocks, lanes), F32), vmem(3))(
        code, received.reshape(devices * cap * 3, lanes), force
    )
    return (jnp.transpose(force, (1, 0, 2)), jnp.transpose(piola, (1, 0, 2)))


def solution(mesh):
    return jax.shard_map(
        per_device,
        mesh=mesh,
        in_specs=(
            P(AXES, None, None),
            P(AXES, None, None),
            P(AXES, None),
            P(AXES, None, None),
            P(AXES),
            P(AXES, None, None),
            P(AXES, None),
            P(AXES, None),
        ),
        out_specs=(P(AXES, None, None), P(AXES, None, None)),
        check_vma=False,
    )
```

```python
import math

import jax
import jax.numpy as jnp
from jax import lax
from jax.experimental import pallas as pl
from jax.experimental.pallas import tpu as pltpu
from jax.sharding import PartitionSpec as P

SH = 4
SUPPORT_SQ = 0.5
CONTACT_SQ = 0.1
PENALTY = 200.0
GROUP = 8
ROWS = 7
SIDE = 48
F32 = jnp.float32
BF16 = jnp.bfloat16
AXES = ("gx", "yz")
NT = (((1,), (1,)), ((), ()))
NN = (((1,), (0,)), ((), ()))


def high(x):
    return x.astype(BF16).astype(F32)


def parts(x, count):
    out = []
    for _ in range(count - 1):
        h = high(x)
        out.append(h)
        x = x - h
    out.append(high(x))
    return out


def mm(a, b, dims):
    return lax.dot_general(a, b, dims, preferred_element_type=F32)


def plan_kernel(owner_hbm, local_hbm, ask_ref, start_ref, owner_ref, local_ref, rows, sem, *, cap):
    copies = [
        pltpu.make_async_copy(owner_hbm, owner_ref, sem.at[0]),
        pltpu.make_async_copy(local_hbm, local_ref, sem.at[1]),
    ]
    for c in copies:
        c.start()
    fanout, blocks = local_ref.shape
    devices, width = ask_ref.shape
    total = fanout * blocks
    earlier = lax.broadcasted_iota(jnp.int32, (total, total), 0) < lax.broadcasted_iota(
        jnp.int32, (total, total), 1
    )
    earlier = earlier.astype(F32).astype(BF16)
    for c in copies:
        c.wait()
    for k in range(fanout):
        cols = pl.ds(k * blocks, blocks)
        rows[0:1, cols] = owner_ref[k]
        rows[1:2, cols] = local_ref[k : k + 1, :]
    owner = rows[0:1, :]
    local = (rows[1:2, :] + 1).astype(F32)
    named = owner == lax.broadcasted_iota(jnp.int32, (devices, total), 0)
    hot = named.astype(F32)
    rank = mm(hot.astype(BF16), earlier, NN)
    lane = lax.broadcasted_iota(jnp.int32, (width, total), 0)
    ask = jnp.zeros((devices, width), F32)
    for s in range(cap):
        chosen = jnp.where(rank == float(s), hot, 0.0).astype(BF16)
        ask = ask + mm(chosen, jnp.where(lane == s, local, 0.0).astype(BF16), NT)
    ask_ref[...] = ask.astype(jnp.int32) - 1
    place = jnp.sum(hot * rank, axis=0, keepdims=True).astype(jnp.int32)
    start_ref[0:1, :] = owner * (cap * ROWS) + place
    start_ref[1:2, :] = owner * (cap * 3) + place


def provide_kernel(ask_ref, data_ref, out, wide, *, cap):
    devices = ask_ref.shape[0]
    depth = data_ref.shape[0]
    lanes = data_ref.shape[1] // ROWS
    blocks = depth // 3
    for s in range(cap):
        wide[pl.ds(s, devices, stride=cap), :] = jnp.broadcast_to(
            ask_ref[:, s : s + 1], (devices, lanes)
        )
    step = 64
    local = lax.broadcasted_iota(jnp.int32, (step, depth), 1) % blocks
    for i in range(devices * cap // step):
        hot = (wide[pl.ds(i * step, step), 0:depth] == local).astype(F32).astype(BF16)
        got = mm(hot, data_ref[...], NN)
        for j in range(step // cap):
            r = i * (step // cap) + j
            for c in range(ROWS):
                out[pl.ds((r * ROWS + c) * cap, cap), :] = got[
                    j * cap : (j + 1) * cap, c * lanes : (c + 1) * lanes
                ]


def own_kernel(pos_ref, disp_ref, weight_ref, at_ref, centre_ref, data_ref, side):
    _, blocks, lanes = pos_ref.shape
    inv = 1.0 / SUPPORT_SQ
    for c in range(ROWS):
        x = weight_ref[...] if c == 6 else (pos_ref if c < 3 else disp_ref)[c % 3]
        data_ref[:, c * lanes : (c + 1) * lanes] = jnp.concatenate(parts(x, 3), axis=0).astype(BF16)
    side[...] = jnp.zeros_like(side)
    centre_ref[...] = jnp.zeros_like(centre_ref)
    ones = jnp.ones((GROUP, lanes), F32)
    for d in (0, 3, 5):
        side[pl.ds(d * 8 + 7, GROUP, stride=SIDE), :] = ones

    def group(g, _):
        start = pl.multiple_of(g * GROUP, GROUP)
        norm = jnp.zeros((GROUP, lanes), F32)
        for c in range(3):
            x = pos_ref[c, pl.ds(start, GROUP), :]
            mid = jnp.broadcast_to(x[:, 0:1], x.shape)
            x = x - mid
            centre_ref[pl.ds(start * 8 + c, GROUP, stride=8), :] = mid
            norm = norm + x * x
            h, m, l = [2.0 * inv * p for p in parts(x, 3)]
            for d, v in enumerate((h, m, l, h, m, h)):
                side[pl.ds(d * 8 + c, GROUP, stride=SIDE), :] = v
        for d, v in enumerate(parts(1.0 - inv * norm, 3)):
            side[pl.ds(d * 8 + 3, GROUP, stride=SIDE), :] = v
        for q in range(GROUP):
            at_ref[start + q] = jnp.transpose(side[pl.ds(q * SIDE, SIDE), :]).astype(BF16)
        return 0

    lax.fori_loop(0, blocks // GROUP, group, 0)


def contact_kernel(
    pos_ref, disp_ref, weight_ref, below_ref, above_ref, pick_ref, force_ref, out_ref, wide, cur
):
    blocks, lanes = weight_ref.shape
    half = below_ref.shape[0]
    for c in range(3):
        cur[c] = pos_ref[c] + disp_ref[c]
    for s in range(2 * half):
        block = below_ref[s] if s < half else above_ref[s - half]
        turned = jnp.transpose(jnp.concatenate([block, block], axis=0))
        for c in range(4):
            wide[s, c] = jnp.broadcast_to(turned[:, c : c + 1], (lanes, lanes))

    def block(b, _):
        own = [jnp.broadcast_to(cur[c, pl.ds(b, 1), :], (8, lanes)) for c in range(3)]
        total = [jnp.zeros((8, lanes), F32) for _ in range(3)]
        for k in range(2):
            s = pick_ref[b, k]
            for r in range(lanes // 8):
                rows = pl.ds(r * 8, 8)
                gap = [own[c] - wide[s, c, rows, :] for c in range(3)]
                near = jnp.maximum(
                    CONTACT_SQ - (gap[0] * gap[0] + gap[1] * gap[1] + gap[2] * gap[2]), 0.0
                )
                push = near * near * wide[s, 3, rows, :]
                total = [total[c] + push * gap[c] for c in range(3)]
        scale = PENALTY * (weight_ref[pl.ds(b, 1), :] > 0).astype(F32)
        for c in range(3):
            push = scale * jnp.sum(total[c], axis=0, keepdims=True)
            out_ref[c, pl.ds(b, 1), :] = force_ref[c, pl.ds(b, 1), :] + push
        return 0

    lax.fori_loop(0, blocks, block, 0)


def main_kernel(
    start_ref, pos_ref, disp_ref, weight_ref, lame_ref, at_ref, centre_ref, got_ref,
    piola_ref, force_ref, back_ref,
    raw, far, b_all, f_all, k_all, ss, gs,
):
    blocks, lanes = weight_ref.shape
    fanout = far.shape[1]
    cap = 4
    coeff = -3.0 / math.sqrt(fanout * lanes)
    inv = 1.0 / SUPPORT_SQ
    back_ref[...] = jnp.zeros_like(back_ref)
    gs[...] = jnp.zeros_like(gs)
    raw[...] = jnp.zeros_like(raw)
    row = lax.broadcasted_iota(jnp.int32, (8, lanes), 0)

    def far_side(b, _):
        centre = centre_ref[pl.ds(pl.multiple_of(b * 8, 8), 8), :]
        for k in range(fanout):
            raw[k, 0:ROWS, :] = got_ref[pl.ds(start_ref[0, k * blocks + b], ROWS, stride=cap), :]
        for k in range(fanout):
            t = raw[k] - centre
            far[b, k] = t
            square = t * t
            norm = square[0:1] + square[1:2] + square[2:3]
            place = jnp.where(row == 3, 1.0, jnp.where(row == 7, -inv * norm, t))
            h, m, l = parts(place, 3)
            cols = pl.ds(k * lanes, lanes)
            b_all[b, :, cols] = jnp.concatenate([h, h, h, m, m, l], axis=0).astype(BF16)
            weight = t[6:7]
            plain = jnp.where(row == 6, 1.0, t)
            feats = [weight * plain] + [(weight * t[3 + a : 4 + a]) * plain for a in range(3)]
            split = [parts(v, 2) for v in feats]
            f_all[b, :, cols] = jnp.concatenate(
                [v[0] for v in split] + [v[1] for v in split], axis=0
            ).astype(BF16)
        return 0


    def forward(g, q):
        turn = g % 2
        b = g * GROUP + q
        far_side(b, 0)
        near = jnp.maximum(mm(at_ref[b], b_all[b], NN), 0.0)
        near = near * near
        hi = near.astype(BF16)
        lo = (near - hi.astype(F32)).astype(BF16)
        k_all[turn * GROUP + q, 0:lanes, :] = hi
        k_all[turn * GROUP + q, lanes:, :] = lo
        feat = f_all[b]
        sums = mm(
            jnp.concatenate([hi, lo], axis=1), jnp.concatenate([feat, feat], axis=1), NT
        )
        sums = jnp.transpose(sums)
        ss[turn, pl.ds(pl.multiple_of(q * 32, 32), 32), :] = sums[0:32] + sums[32:64]

    def middle(g):
        turn = g % 2
        rows = pl.ds(pl.multiple_of(g * GROUP, GROUP), GROUP)

        def total(f):
            return ss[turn, pl.ds(f, GROUP, stride=32), :]

        mass = total(6)
        weight = weight_ref[rows, :]
        inside = (weight > 0).astype(F32)
        here = [pos_ref[c, rows, :] for c in range(3)]
        here = [x - x[:, 0:1] for x in here]
        moved = [disp_ref[c, rows, :] for c in range(3)]
        column = [coeff * (here[c] * mass - total(c)) for c in range(3)]
        deform = [
            [
                (1.0 if a == c else 0.0)
                + coeff * (here[c] * total(3 + a) - total(8 + 8 * a + c))
                - moved[a] * column[c]
                for c in range(3)
            ]
            for a in range(3)
        ]
        strain = [[None] * 3 for _ in range(3)]
        for a in range(3):
            for c in range(a, 3):
                v = sum(deform[k][a] * deform[k][c] for k in range(3))
                strain[a][c] = strain[c][a] = 0.5 * (v - (1.0 if a == c else 0.0))
        trace = lame_ref[0, rows, :] * (strain[0][0] + strain[1][1] + strain[2][2])
        twice = 2.0 * lame_ref[1, rows, :]
        second = [
            [(trace if a == c else 0.0) + twice * strain[a][c] for c in range(3)] for a in range(3)
        ]
        scaled = [[None] * 3 for _ in range(3)]
        for a in range(3):
            for c in range(3):
                v = sum(deform[a][k] * second[k][c] for k in range(3)) * inside
                piola_ref[3 * a + c, rows, :] = v
                scaled[a][c] = weight * v
        for a in range(3):
            own = sum(scaled[a][c] * column[c] for c in range(3))
            force_ref[a, rows, :] = own
            feats = scaled[a] + [sum(scaled[a][c] * here[c] for c in range(3))]
            for f, v in enumerate(feats):
                h, l = parts(v, 2)
                gs[turn, pl.ds(f * 8 + a, GROUP, stride=32), :] = h
                gs[turn, pl.ds(f * 8 + 4 + a, GROUP, stride=32), :] = l

    def backward(g, q):
        turn = g % 2
        b = g * GROUP + q
        feat = gs[turn, pl.ds(pl.multiple_of(q * 32, 32), 32), :].astype(BF16)
        feat = jnp.concatenate([feat, feat], axis=1)
        for k in range(0, fanout, 2):
            sums = mm(feat, k_all[turn * GROUP + q, :, pl.ds(k * lanes, 2 * lanes)], NN)
            for j in range(2):
                back = [sums[8 * f : 8 * f + 8, j * lanes : (j + 1) * lanes] for f in range(4)]
                cast = [far[b, k + j, pl.ds(c, 8, stride=0), :] for c in (0, 1, 2, 6)]
                v = back[3] - sum(cast[c] * back[c] for c in range(3))
                v = (-coeff * cast[3]) * v
                first = start_ref[1, (k + j) * blocks + b]
                back_ref[pl.ds(first, 3, stride=cap), :] = v[0:3] + v[4:7]

    def first(q, _):
        forward(0, q)
        return 0

    def both(g, _):
        def block(q, _):
            forward(g, q)
            backward(g - 1, q)
            return 0

        lax.fori_loop(0, GROUP, block, 0, unroll=GROUP)
        middle(g)
        return 0

    def last(q, _):
        backward(groups - 1, q)
        return 0

    groups = blocks // GROUP
    lax.fori_loop(0, GROUP, first, 0, unroll=GROUP)
    middle(0)
    lax.fori_loop(1, groups, both, 0, unroll=3)
    lax.fori_loop(0, GROUP, last, 0, unroll=GROUP)


def returned_kernel(code_ref, got_ref, force_ref, out_ref):
    comps, blocks, lanes = force_ref.shape
    rows = got_ref.shape[0]
    target = lax.broadcasted_iota(jnp.int32, (comps * blocks, rows), 0)
    chosen = (target == code_ref[...]).astype(F32).astype(BF16)
    out = force_ref[...].reshape(comps * blocks, lanes)
    for part in parts(got_ref[...], 2):
        out = out + mm(chosen, part.astype(BF16), NN)
    out_ref[...] = out.reshape(comps, blocks, lanes)


def vmem(count):
    return [pl.BlockSpec(memory_space=pltpu.VMEM)] * count


SMEM = pl.BlockSpec(memory_space=pltpu.SMEM)
ANY = pl.BlockSpec(memory_space=pl.ANY)


def call(body, name, out, in_specs, scratch=(), kib=8192, flops=1_000_000, size=1_000_000):
    many = isinstance(out, tuple)
    return pl.pallas_call(
        body,
        out_shape=out,
        in_specs=in_specs,
        out_specs=tuple(vmem(len(out))) if many else vmem(1)[0],
        scratch_shapes=list(scratch),
        compiler_params=pltpu.CompilerParams(vmem_limit_bytes=kib * 2**10),
        cost_estimate=pl.CostEstimate(flops=flops, bytes_accessed=size, transcendentals=0),
        name=name,
    )


def main_call(start, pos_t, disp_t, weight, lame_t, at, centre, got):
    blocks, lanes = weight.shape
    fanout = start.shape[1] // blocks
    wide = fanout * lanes
    back = got.shape[0] // ROWS * 3
    return call(
        main_kernel,
        "pairs",
        (
            jax.ShapeDtypeStruct((9, blocks, lanes), F32),
            jax.ShapeDtypeStruct((3, blocks, lanes), F32),
            jax.ShapeDtypeStruct((back, lanes), F32),
        ),
        [SMEM] + vmem(7),
        [
            pltpu.VMEM((fanout, 8, lanes), F32),
            pltpu.VMEM((blocks, fanout, 8, lanes), F32),
            pltpu.VMEM((blocks, SIDE, wide), BF16),
            pltpu.VMEM((blocks, 64, wide), BF16),
            pltpu.VMEM((2 * GROUP, 2 * lanes, wide), BF16),
            pltpu.VMEM((2, GROUP * 32, lanes), F32),
            pltpu.VMEM((2, GROUP * 32, lanes), F32),
        ],
        kib=36000,
        flops=60_000_000,
        size=4_000_000,
    )(start, pos_t, disp_t, weight, lame_t, at, centre, got)


def per_device(ref_pos, disp, volume, lame, pad_count, nbr_owner, nbr_local, contact_block):
    blocks, _, lanes = ref_pos.shape
    fanout = nbr_local.shape[1]
    across = lax.axis_size("gx")
    deep = lax.axis_size("yz")
    devices = across * deep
    cap = 2 * blocks * fanout // devices
    total = blocks * fanout
    shape = jax.ShapeDtypeStruct

    ask, start = call(
        lambda *refs: plan_kernel(*refs, cap=cap),
        "plan",
        (shape((devices, 16), jnp.int32), shape((2, total), jnp.int32)),
        [ANY] * 2,
        [
            pltpu.VMEM((fanout, 1, blocks), jnp.int32),
            pltpu.VMEM((fanout, blocks), jnp.int32),
            pltpu.VMEM((8, total), jnp.int32),
            pltpu.SemaphoreType.DMA((2,)),
        ],
        kib=65472,
    )(jnp.transpose(nbr_owner, (1, 2, 0)), jnp.transpose(nbr_local))
    asked = lax.all_to_all(ask, AXES, split_axis=0, concat_axis=0, tiled=True)

    usable = (jnp.arange(lanes)[None, :] < (lanes - pad_count)[:, None]).astype(F32)
    weight = volume * usable
    pos_t = jnp.transpose(ref_pos, (1, 0, 2))
    disp_t = jnp.transpose(disp, (1, 0, 2))
    lame_t = jnp.transpose(lame, (1, 0, 2))

    surface = jnp.concatenate([ref_pos + disp, weight[:, None, :]], axis=1)
    up = [(i, i + 1) for i in range(across - 1)]
    down = [(i + 1, i) for i in range(across - 1)]
    below = lax.ppermute(surface[blocks - SH :], "gx", up)
    above = lax.ppermute(surface[:SH], "gx", down)
    local = contact_block % blocks
    row = contact_block // blocks // deep
    pick = jnp.where(row < lax.axis_index("gx"), local - (blocks - SH), SH + local)

    at, centre, data = call(
        own_kernel,
        "own",
        (
            shape((blocks, lanes, SIDE), BF16),
            shape((blocks * 8, lanes), F32),
            shape((3 * blocks, ROWS * lanes), BF16),
        ),
        vmem(3),
        [pltpu.VMEM((GROUP * SIDE, lanes), F32)],
    )(pos_t, disp_t, weight)

    picked = call(
        lambda *refs: provide_kernel(*refs, cap=cap),
        "provide",
        shape((devices * cap * ROWS, lanes), F32),
        vmem(2),
        [pltpu.VMEM((devices * cap, lanes), jnp.int32)],
    )(asked, data)
    got = lax.all_to_all(
        picked.reshape(devices, ROWS, cap, lanes), AXES, split_axis=0, concat_axis=0, tiled=True
    ).reshape(devices * cap * ROWS, lanes)

    piola, force, back = main_call(start, pos_t, disp_t, weight, lame_t, at, centre, got)
    received = lax.all_to_all(
        back.reshape(devices, 3, cap, lanes), AXES, split_axis=0, concat_axis=0, tiled=True
    )
    force = call(
        contact_kernel,
        "contact",
        shape((3, blocks, lanes), F32),
        vmem(5) + [SMEM] + vmem(1),
        [pltpu.VMEM((2 * SH, 4, lanes, lanes), F32), pltpu.VMEM((3, blocks, lanes), F32)],
        flops=20_000_000,
    )(pos_t, disp_t, weight, below, above, pick, force)
    ids = asked[:, None, 0:cap]
    code = jnp.where(ids >= 0, ids + blocks * jnp.arange(3)[None, :, None], -1).reshape(1, -1)
    force = call(returned_kernel, "returned", shape((3, blocks, lanes), F32), vmem(3))(
        code, received.reshape(devices * cap * 3, lanes), force
    )
    return (jnp.transpose(force, (1, 0, 2)), jnp.transpose(piola, (1, 0, 2)))


def solution(mesh):
    return jax.shard_map(
        per_device,
        mesh=mesh,
        in_specs=(
            P(AXES, None, None),
            P(AXES, None, None),
            P(AXES, None),
            P(AXES, None, None),
            P(AXES),
            P(AXES, None, None),
            P(AXES, None),
            P(AXES, None),
        ),
        out_specs=(P(AXES, None, None), P(AXES, None, None)),
        check_vma=False,
    )
```

```python
import math

import jax
import jax.numpy as jnp
from jax import lax
from jax.experimental import pallas as pl
from jax.experimental.pallas import tpu as pltpu
from jax.sharding import PartitionSpec as P

SH = 4
SUPPORT_SQ = 0.5
CONTACT_SQ = 0.1
PENALTY = 200.0
GROUP = 8
ROWS = 7
SIDE = 48
F32 = jnp.float32
BF16 = jnp.bfloat16
AXES = ("gx", "yz")
NT = (((1,), (1,)), ((), ()))
NN = (((1,), (0,)), ((), ()))


def high(x):
    return x.astype(BF16).astype(F32)


def parts(x, count):
    out = []
    for _ in range(count - 1):
        h = high(x)
        out.append(h)
        x = x - h
    out.append(high(x))
    return out


def mm(a, b, dims):
    return lax.dot_general(a, b, dims, preferred_element_type=F32)


def plan_kernel(owner_hbm, local_hbm, ask_ref, start_ref, owner_ref, local_ref, rows, sem, *, cap):
    copies = [
        pltpu.make_async_copy(owner_hbm, owner_ref, sem.at[0]),
        pltpu.make_async_copy(local_hbm, local_ref, sem.at[1]),
    ]
    for c in copies:
        c.start()
    fanout, blocks = local_ref.shape
    devices, width = ask_ref.shape
    total = fanout * blocks
    earlier = lax.broadcasted_iota(jnp.int32, (total, total), 0) < lax.broadcasted_iota(
        jnp.int32, (total, total), 1
    )
    earlier = earlier.astype(F32).astype(BF16)
    for c in copies:
        c.wait()
    for k in range(fanout):
        cols = pl.ds(k * blocks, blocks)
        rows[0:1, cols] = owner_ref[k]
        rows[1:2, cols] = local_ref[k : k + 1, :]
    owner = rows[0:1, :]
    local = (rows[1:2, :] + 1).astype(F32)
    named = owner == lax.broadcasted_iota(jnp.int32, (devices, total), 0)
    hot = named.astype(F32)
    rank = mm(hot.astype(BF16), earlier, NN)
    lane = lax.broadcasted_iota(jnp.int32, (width, total), 0)
    ask = jnp.zeros((devices, width), F32)
    for s in range(cap):
        chosen = jnp.where(rank == float(s), hot, 0.0).astype(BF16)
        ask = ask + mm(chosen, jnp.where(lane == s, local, 0.0).astype(BF16), NT)
    ask_ref[...] = ask.astype(jnp.int32) - 1
    place = jnp.sum(hot * rank, axis=0, keepdims=True).astype(jnp.int32)
    start_ref[0:1, :] = owner * (cap * ROWS) + place
    start_ref[1:2, :] = owner * (cap * 3) + place


def provide_kernel(ask_ref, data_ref, out, wide, *, cap):
    devices = ask_ref.shape[0]
    depth = data_ref.shape[0]
    lanes = data_ref.shape[1] // ROWS
    blocks = depth // 3
    for s in range(cap):
        wide[pl.ds(s, devices, stride=cap), :] = jnp.broadcast_to(
            ask_ref[:, s : s + 1], (devices, lanes)
        )
    step = 64
    local = lax.broadcasted_iota(jnp.int32, (step, depth), 1) % blocks
    for i in range(devices * cap // step):
        hot = (wide[pl.ds(i * step, step), 0:depth] == local).astype(F32).astype(BF16)
        got = mm(hot, data_ref[...], NN)
        for j in range(step // cap):
            r = i * (step // cap) + j
            for c in range(ROWS):
                out[pl.ds((r * ROWS + c) * cap, cap), :] = got[
                    j * cap : (j + 1) * cap, c * lanes : (c + 1) * lanes
                ]


def own_kernel(pos_ref, disp_ref, weight_ref, at_ref, centre_ref, data_ref, side):
    _, blocks, lanes = pos_ref.shape
    inv = 1.0 / SUPPORT_SQ
    for c in range(ROWS):
        x = weight_ref[...] if c == 6 else (pos_ref if c < 3 else disp_ref)[c % 3]
        data_ref[:, c * lanes : (c + 1) * lanes] = jnp.concatenate(parts(x, 3), axis=0).astype(BF16)
    side[...] = jnp.zeros_like(side)
    centre_ref[...] = jnp.zeros_like(centre_ref)
    ones = jnp.ones((GROUP, lanes), F32)
    for d in (0, 3, 5):
        side[pl.ds(d * 8 + 7, GROUP, stride=SIDE), :] = ones

    def group(g, _):
        start = pl.multiple_of(g * GROUP, GROUP)
        norm = jnp.zeros((GROUP, lanes), F32)
        for c in range(3):
            x = pos_ref[c, pl.ds(start, GROUP), :]
            mid = jnp.broadcast_to(x[:, 0:1], x.shape)
            x = x - mid
            centre_ref[pl.ds(start * 8 + c, GROUP, stride=8), :] = mid
            norm = norm + x * x
            h, m, l = [2.0 * inv * p for p in parts(x, 3)]
            for d, v in enumerate((h, m, l, h, m, h)):
                side[pl.ds(d * 8 + c, GROUP, stride=SIDE), :] = v
        for d, v in enumerate(parts(1.0 - inv * norm, 3)):
            side[pl.ds(d * 8 + 3, GROUP, stride=SIDE), :] = v
        for q in range(GROUP):
            at_ref[start + q] = jnp.transpose(side[pl.ds(q * SIDE, SIDE), :]).astype(BF16)
        return 0

    lax.fori_loop(0, blocks // GROUP, group, 0)


def contact_kernel(
    pos_ref, disp_ref, weight_ref, below_ref, above_ref, pick_ref, force_ref, out_ref, wide, cur
):
    blocks, lanes = weight_ref.shape
    half = below_ref.shape[0]
    for c in range(3):
        cur[c] = pos_ref[c] + disp_ref[c]
    for s in range(2 * half):
        block = below_ref[s] if s < half else above_ref[s - half]
        turned = jnp.transpose(jnp.concatenate([block, block], axis=0))
        for c in range(4):
            wide[s, c] = jnp.broadcast_to(turned[:, c : c + 1], (lanes, lanes))

    def block(b, _):
        own = [jnp.broadcast_to(cur[c, pl.ds(b, 1), :], (8, lanes)) for c in range(3)]
        total = [jnp.zeros((8, lanes), F32) for _ in range(3)]
        for k in range(2):
            s = pick_ref[b, k]
            for r in range(lanes // 8):
                rows = pl.ds(r * 8, 8)
                gap = [own[c] - wide[s, c, rows, :] for c in range(3)]
                near = jnp.maximum(
                    CONTACT_SQ - (gap[0] * gap[0] + gap[1] * gap[1] + gap[2] * gap[2]), 0.0
                )
                push = near * near * wide[s, 3, rows, :]
                total = [total[c] + push * gap[c] for c in range(3)]
        scale = PENALTY * (weight_ref[pl.ds(b, 1), :] > 0).astype(F32)
        for c in range(3):
            push = scale * jnp.sum(total[c], axis=0, keepdims=True)
            out_ref[c, pl.ds(b, 1), :] = force_ref[c, pl.ds(b, 1), :] + push
        return 0

    lax.fori_loop(0, blocks, block, 0)


def main_kernel(
    start_ref, pos_ref, disp_ref, weight_ref, lame_ref, at_ref, centre_ref, got_ref,
    piola_ref, force_ref, back_ref,
    raw, far, b_all, f_all, k_all, ss, gs,
):
    blocks, lanes = weight_ref.shape
    fanout = far.shape[1]
    cap = 4
    coeff = -3.0 / math.sqrt(fanout * lanes)
    inv = 1.0 / SUPPORT_SQ
    back_ref[...] = jnp.zeros_like(back_ref)
    gs[...] = jnp.zeros_like(gs)
    raw[...] = jnp.zeros_like(raw)
    row = lax.broadcasted_iota(jnp.int32, (8, lanes), 0)

    def far_side(b, _):
        centre = centre_ref[pl.ds(pl.multiple_of(b * 8, 8), 8), :]
        for k in range(fanout):
            raw[k, 0:ROWS, :] = got_ref[pl.ds(start_ref[0, k * blocks + b], ROWS, stride=cap), :]
        for k in range(fanout):
            t = raw[k] - centre
            far[b, k] = t
            square = t * t
            norm = square[0:1] + square[1:2] + square[2:3]
            place = jnp.where(row == 3, 1.0, jnp.where(row == 7, -inv * norm, t))
            h, m, l = parts(place, 3)
            cols = pl.ds(k * lanes, lanes)
            b_all[b, :, cols] = jnp.concatenate([h, h, h, m, m, l], axis=0).astype(BF16)
            weight = raw[k, pl.ds(6, 8, stride=0), :]
            heavy = weight * jnp.where(row == 6, 1.0, t)
            feats = [heavy] + [raw[k, pl.ds(3 + a, 8, stride=0), :] * heavy for a in range(3)]
            split = [parts(v, 2) for v in feats]
            f_all[b, :, cols] = jnp.concatenate(
                [v[0] for v in split] + [v[1] for v in split], axis=0
            ).astype(BF16)
        return 0


    def forward(g, q):
        turn = g % 2
        b = g * GROUP + q
        far_side(b, 0)
        near = jnp.maximum(mm(at_ref[b], b_all[b], NN), 0.0)
        near = near * near
        hi = near.astype(BF16)
        lo = (near - hi.astype(F32)).astype(BF16)
        k_all[turn * GROUP + q, 0:lanes, :] = hi
        k_all[turn * GROUP + q, lanes:, :] = lo
        feat = f_all[b]
        sums = mm(
            jnp.concatenate([hi, lo], axis=1), jnp.concatenate([feat, feat], axis=1), NT
        )
        sums = jnp.transpose(sums)
        ss[turn, pl.ds(pl.multiple_of(q * 32, 32), 32), :] = sums[0:32] + sums[32:64]

    def middle(g):
        turn = g % 2
        rows = pl.ds(pl.multiple_of(g * GROUP, GROUP), GROUP)

        def total(f):
            return ss[turn, pl.ds(f, GROUP, stride=32), :]

        mass = total(6)
        weight = weight_ref[rows, :]
        inside = (weight > 0).astype(F32)
        here = [pos_ref[c, rows, :] for c in range(3)]
        here = [x - x[:, 0:1] for x in here]
        moved = [disp_ref[c, rows, :] for c in range(3)]
        column = [coeff * (here[c] * mass - total(c)) for c in range(3)]
        deform = [
            [
                (1.0 if a == c else 0.0)
                + coeff * (here[c] * total(3 + a) - total(8 + 8 * a + c))
                - moved[a] * column[c]
                for c in range(3)
            ]
            for a in range(3)
        ]
        strain = [[None] * 3 for _ in range(3)]
        for a in range(3):
            for c in range(a, 3):
                v = sum(deform[k][a] * deform[k][c] for k in range(3))
                strain[a][c] = strain[c][a] = 0.5 * (v - (1.0 if a == c else 0.0))
        trace = lame_ref[0, rows, :] * (strain[0][0] + strain[1][1] + strain[2][2])
        twice = 2.0 * lame_ref[1, rows, :]
        second = [
            [(trace if a == c else 0.0) + twice * strain[a][c] for c in range(3)] for a in range(3)
        ]
        scaled = [[None] * 3 for _ in range(3)]
        for a in range(3):
            for c in range(3):
                v = sum(deform[a][k] * second[k][c] for k in range(3)) * inside
                piola_ref[3 * a + c, rows, :] = v
                scaled[a][c] = weight * v
        for a in range(3):
            own = sum(scaled[a][c] * column[c] for c in range(3))
            force_ref[a, rows, :] = own
            feats = scaled[a] + [sum(scaled[a][c] * here[c] for c in range(3))]
            for f, v in enumerate(feats):
                h, l = parts(v, 2)
                gs[turn, pl.ds(f * 8 + a, GROUP, stride=32), :] = h
                gs[turn, pl.ds(f * 8 + 4 + a, GROUP, stride=32), :] = l

    def backward(g, q):
        turn = g % 2
        b = g * GROUP + q
        feat = gs[turn, pl.ds(pl.multiple_of(q * 32, 32), 32), :].astype(BF16)
        feat = jnp.concatenate([feat, feat], axis=1)
        for k in range(0, fanout, 2):
            sums = mm(feat, k_all[turn * GROUP + q, :, pl.ds(k * lanes, 2 * lanes)], NN)
            for j in range(2):
                back = [sums[8 * f : 8 * f + 8, j * lanes : (j + 1) * lanes] for f in range(4)]
                cast = [far[b, k + j, pl.ds(c, 8, stride=0), :] for c in (0, 1, 2, 6)]
                v = back[3] - sum(cast[c] * back[c] for c in range(3))
                v = (-coeff * cast[3]) * v
                first = start_ref[1, (k + j) * blocks + b]
                back_ref[pl.ds(first, 3, stride=cap), :] = v[0:3] + v[4:7]

    def first(q, _):
        forward(0, q)
        return 0

    def both(g, _):
        for q in range(2):
            forward(g, q)
        middle(g - 1)
        for q in range(2, GROUP):
            forward(g, q)
            backward(g - 1, q - 2)
        for q in range(GROUP - 2, GROUP):
            backward(g - 1, q)
        return 0

    def last(q, _):
        backward(groups - 1, q)
        return 0

    groups = blocks // GROUP
    lax.fori_loop(0, GROUP, first, 0, unroll=GROUP)
    lax.fori_loop(1, groups, both, 0, unroll=groups - 1)
    middle(groups - 1)
    lax.fori_loop(0, GROUP, last, 0, unroll=GROUP)


def returned_kernel(code_ref, got_ref, force_ref, out_ref):
    comps, blocks, lanes = force_ref.shape
    rows = got_ref.shape[0]
    target = lax.broadcasted_iota(jnp.int32, (comps * blocks, rows), 0)
    chosen = (target == code_ref[...]).astype(F32).astype(BF16)
    out = force_ref[...].reshape(comps * blocks, lanes)
    for part in parts(got_ref[...], 2):
        out = out + mm(chosen, part.astype(BF16), NN)
    out_ref[...] = out.reshape(comps, blocks, lanes)


def vmem(count):
    return [pl.BlockSpec(memory_space=pltpu.VMEM)] * count


SMEM = pl.BlockSpec(memory_space=pltpu.SMEM)
ANY = pl.BlockSpec(memory_space=pl.ANY)


def call(body, name, out, in_specs, scratch=(), kib=8192, flops=1_000_000, size=1_000_000):
    many = isinstance(out, tuple)
    return pl.pallas_call(
        body,
        out_shape=out,
        in_specs=in_specs,
        out_specs=tuple(vmem(len(out))) if many else vmem(1)[0],
        scratch_shapes=list(scratch),
        compiler_params=pltpu.CompilerParams(vmem_limit_bytes=kib * 2**10),
        cost_estimate=pl.CostEstimate(flops=flops, bytes_accessed=size, transcendentals=0),
        name=name,
    )


def main_call(start, pos_t, disp_t, weight, lame_t, at, centre, got):
    blocks, lanes = weight.shape
    fanout = start.shape[1] // blocks
    wide = fanout * lanes
    back = got.shape[0] // ROWS * 3
    return call(
        main_kernel,
        "pairs",
        (
            jax.ShapeDtypeStruct((9, blocks, lanes), F32),
            jax.ShapeDtypeStruct((3, blocks, lanes), F32),
            jax.ShapeDtypeStruct((back, lanes), F32),
        ),
        [SMEM] + vmem(7),
        [
            pltpu.VMEM((fanout, 8, lanes), F32),
            pltpu.VMEM((blocks, fanout, 8, lanes), F32),
            pltpu.VMEM((blocks, SIDE, wide), BF16),
            pltpu.VMEM((blocks, 64, wide), BF16),
            pltpu.VMEM((2 * GROUP, 2 * lanes, wide), BF16),
            pltpu.VMEM((2, GROUP * 32, lanes), F32),
            pltpu.VMEM((2, GROUP * 32, lanes), F32),
        ],
        kib=36000,
        flops=60_000_000,
        size=4_000_000,
    )(start, pos_t, disp_t, weight, lame_t, at, centre, got)


def per_device(ref_pos, disp, volume, lame, pad_count, nbr_owner, nbr_local, contact_block):
    blocks, _, lanes = ref_pos.shape
    fanout = nbr_local.shape[1]
    across = lax.axis_size("gx")
    deep = lax.axis_size("yz")
    devices = across * deep
    cap = 2 * blocks * fanout // devices
    total = blocks * fanout
    shape = jax.ShapeDtypeStruct

    ask, start = call(
        lambda *refs: plan_kernel(*refs, cap=cap),
        "plan",
        (shape((devices, 16), jnp.int32), shape((2, total), jnp.int32)),
        [ANY] * 2,
        [
            pltpu.VMEM((fanout, 1, blocks), jnp.int32),
            pltpu.VMEM((fanout, blocks), jnp.int32),
            pltpu.VMEM((8, total), jnp.int32),
            pltpu.SemaphoreType.DMA((2,)),
        ],
        kib=65472,
    )(jnp.transpose(nbr_owner, (1, 2, 0)), jnp.transpose(nbr_local))
    asked = lax.all_to_all(ask, AXES, split_axis=0, concat_axis=0, tiled=True)

    usable = (jnp.arange(lanes)[None, :] < (lanes - pad_count)[:, None]).astype(F32)
    weight = volume * usable
    pos_t = jnp.transpose(ref_pos, (1, 0, 2))
    disp_t = jnp.transpose(disp, (1, 0, 2))
    lame_t = jnp.transpose(lame, (1, 0, 2))

    surface = jnp.concatenate([ref_pos + disp, weight[:, None, :]], axis=1)
    up = [(i, i + 1) for i in range(across - 1)]
    down = [(i + 1, i) for i in range(across - 1)]
    below = lax.ppermute(surface[blocks - SH :], "gx", up)
    above = lax.ppermute(surface[:SH], "gx", down)
    local = contact_block % blocks
    row = contact_block // blocks // deep
    pick = jnp.where(row < lax.axis_index("gx"), local - (blocks - SH), SH + local)

    at, centre, data = call(
        own_kernel,
        "own",
        (
            shape((blocks, lanes, SIDE), BF16),
            shape((blocks * 8, lanes), F32),
            shape((3 * blocks, ROWS * lanes), BF16),
        ),
        vmem(3),
        [pltpu.VMEM((GROUP * SIDE, lanes), F32)],
    )(pos_t, disp_t, weight)

    picked = call(
        lambda *refs: provide_kernel(*refs, cap=cap),
        "provide",
        shape((devices * cap * ROWS, lanes), F32),
        vmem(2),
        [pltpu.VMEM((devices * cap, lanes), jnp.int32)],
    )(asked, data)
    got = lax.all_to_all(
        picked.reshape(devices, ROWS, cap, lanes), AXES, split_axis=0, concat_axis=0, tiled=True
    ).reshape(devices * cap * ROWS, lanes)

    piola, force, back = main_call(start, pos_t, disp_t, weight, lame_t, at, centre, got)
    received = lax.all_to_all(
        back.reshape(devices, 3, cap, lanes), AXES, split_axis=0, concat_axis=0, tiled=True
    )
    force = call(
        contact_kernel,
        "contact",
        shape((3, blocks, lanes), F32),
        vmem(5) + [SMEM] + vmem(1),
        [pltpu.VMEM((2 * SH, 4, lanes, lanes), F32), pltpu.VMEM((3, blocks, lanes), F32)],
        flops=20_000_000,
    )(pos_t, disp_t, weight, below, above, pick, force)
    ids = asked[:, None, 0:cap]
    code = jnp.where(ids >= 0, ids + blocks * jnp.arange(3)[None, :, None], -1).reshape(1, -1)
    force = call(returned_kernel, "returned", shape((3, blocks, lanes), F32), vmem(3))(
        code, received.reshape(devices * cap * 3, lanes), force
    )
    return (jnp.transpose(force, (1, 0, 2)), jnp.transpose(piola, (1, 0, 2)))


def solution(mesh):
    return jax.shard_map(
        per_device,
        mesh=mesh,
        in_specs=(
            P(AXES, None, None),
            P(AXES, None, None),
            P(AXES, None),
            P(AXES, None, None),
            P(AXES),
            P(AXES, None, None),
            P(AXES, None),
            P(AXES, None),
        ),
        out_specs=(P(AXES, None, None), P(AXES, None, None)),
        check_vma=False,
    )
```

```python
import math

import jax
import jax.numpy as jnp
from jax import lax
from jax.experimental import pallas as pl
from jax.experimental.pallas import tpu as pltpu
from jax.sharding import PartitionSpec as P

SH = 4
SUPPORT_SQ = 0.5
CONTACT_SQ = 0.1
PENALTY = 200.0
GROUP = 8
ROWS = 7
SIDE = 48
F32 = jnp.float32
BF16 = jnp.bfloat16
AXES = ("gx", "yz")
NT = (((1,), (1,)), ((), ()))
NN = (((1,), (0,)), ((), ()))


def high(x):
    return x.astype(BF16).astype(F32)


def parts(x, count):
    out = []
    for _ in range(count - 1):
        h = high(x)
        out.append(h)
        x = x - h
    out.append(high(x))
    return out


def mm(a, b, dims):
    return lax.dot_general(a, b, dims, preferred_element_type=F32)


def plan_kernel(owner_hbm, local_hbm, ask_ref, start_ref, owner_ref, local_ref, rows, sem, *, cap):
    copies = [
        pltpu.make_async_copy(owner_hbm, owner_ref, sem.at[0]),
        pltpu.make_async_copy(local_hbm, local_ref, sem.at[1]),
    ]
    for c in copies:
        c.start()
    fanout, blocks = local_ref.shape
    devices, width = ask_ref.shape
    total = fanout * blocks
    earlier = lax.broadcasted_iota(jnp.int32, (total, total), 0) < lax.broadcasted_iota(
        jnp.int32, (total, total), 1
    )
    earlier = earlier.astype(F32).astype(BF16)
    for c in copies:
        c.wait()
    for k in range(fanout):
        cols = pl.ds(k * blocks, blocks)
        rows[0:1, cols] = owner_ref[k]
        rows[1:2, cols] = local_ref[k : k + 1, :]
    owner = rows[0:1, :]
    local = (rows[1:2, :] + 1).astype(F32)
    named = owner == lax.broadcasted_iota(jnp.int32, (devices, total), 0)
    hot = named.astype(F32)
    rank = mm(hot.astype(BF16), earlier, NN)
    place = jnp.sum(hot * rank, axis=0, keepdims=True)
    lane = lax.broadcasted_iota(jnp.int32, (width, total), 0).astype(F32)
    chosen = jnp.where(lane == place, local, 0.0).astype(BF16)
    ask_ref[...] = mm(hot.astype(BF16), chosen, NT).astype(jnp.int32) - 1
    place = place.astype(jnp.int32)
    start_ref[0:1, :] = owner * (cap * ROWS) + place
    start_ref[1:2, :] = owner * (cap * 3) + place


def provide_kernel(ask_ref, data_ref, out, wide, *, cap):
    devices = ask_ref.shape[0]
    depth = data_ref.shape[0]
    lanes = data_ref.shape[1] // ROWS
    blocks = depth // 3
    for s in range(cap):
        wide[pl.ds(s, devices, stride=cap), :] = jnp.broadcast_to(
            ask_ref[:, s : s + 1], (devices, lanes)
        )
    step = 64
    local = lax.broadcasted_iota(jnp.int32, (step, depth), 1) % blocks
    for i in range(devices * cap // step):
        hot = (wide[pl.ds(i * step, step), 0:depth] == local).astype(F32).astype(BF16)
        got = mm(hot, data_ref[...], NN)
        for j in range(step // cap):
            r = i * (step // cap) + j
            for c in range(ROWS):
                out[pl.ds((r * ROWS + c) * cap, cap), :] = got[
                    j * cap : (j + 1) * cap, c * lanes : (c + 1) * lanes
                ]


def own_kernel(pos_ref, disp_ref, weight_ref, at_ref, centre_ref, data_ref, side):
    _, blocks, lanes = pos_ref.shape
    inv = 1.0 / SUPPORT_SQ
    for c in range(ROWS):
        x = weight_ref[...] if c == 6 else (pos_ref if c < 3 else disp_ref)[c % 3]
        data_ref[:, c * lanes : (c + 1) * lanes] = jnp.concatenate(parts(x, 3), axis=0).astype(BF16)
    side[...] = jnp.zeros_like(side)
    centre_ref[...] = jnp.zeros_like(centre_ref)
    ones = jnp.ones((GROUP, lanes), F32)
    for d in (0, 3, 5):
        side[pl.ds(d * 8 + 7, GROUP, stride=SIDE), :] = ones

    def group(g, _):
        start = pl.multiple_of(g * GROUP, GROUP)
        norm = jnp.zeros((GROUP, lanes), F32)
        for c in range(3):
            x = pos_ref[c, pl.ds(start, GROUP), :]
            mid = jnp.broadcast_to(x[:, 0:1], x.shape)
            x = x - mid
            centre_ref[pl.ds(start * 8 + c, GROUP, stride=8), :] = mid
            norm = norm + x * x
            h, m, l = [2.0 * inv * p for p in parts(x, 3)]
            for d, v in enumerate((h, m, l, h, m, h)):
                side[pl.ds(d * 8 + c, GROUP, stride=SIDE), :] = v
        for d, v in enumerate(parts(1.0 - inv * norm, 3)):
            side[pl.ds(d * 8 + 3, GROUP, stride=SIDE), :] = v
        for q in range(GROUP):
            at_ref[start + q] = jnp.transpose(side[pl.ds(q * SIDE, SIDE), :]).astype(BF16)
        return 0

    lax.fori_loop(0, blocks // GROUP, group, 0)


def contact_kernel(
    pos_ref, disp_ref, weight_ref, below_ref, above_ref, pick_ref, force_ref, out_ref, wide, cur
):
    blocks, lanes = weight_ref.shape
    half = below_ref.shape[0]
    for c in range(3):
        cur[c] = pos_ref[c] + disp_ref[c]
    for s in range(2 * half):
        block = below_ref[s] if s < half else above_ref[s - half]
        turned = jnp.transpose(jnp.concatenate([block, block], axis=0))
        for c in range(4):
            wide[s, c] = jnp.broadcast_to(turned[:, c : c + 1], (lanes, lanes))

    def block(b, _):
        own = [jnp.broadcast_to(cur[c, pl.ds(b, 1), :], (8, lanes)) for c in range(3)]
        total = [jnp.zeros((8, lanes), F32) for _ in range(3)]
        for k in range(2):
            s = pick_ref[b, k]
            for r in range(lanes // 8):
                rows = pl.ds(r * 8, 8)
                gap = [own[c] - wide[s, c, rows, :] for c in range(3)]
                near = jnp.maximum(
                    CONTACT_SQ - (gap[0] * gap[0] + gap[1] * gap[1] + gap[2] * gap[2]), 0.0
                )
                push = near * near * wide[s, 3, rows, :]
                total = [total[c] + push * gap[c] for c in range(3)]
        scale = PENALTY * (weight_ref[pl.ds(b, 1), :] > 0).astype(F32)
        for c in range(3):
            push = scale * jnp.sum(total[c], axis=0, keepdims=True)
            out_ref[c, pl.ds(b, 1), :] = force_ref[c, pl.ds(b, 1), :] + push
        return 0

    lax.fori_loop(0, blocks, block, 0)


def main_kernel(
    start_ref, pos_ref, disp_ref, weight_ref, lame_ref, at_ref, centre_ref, got_ref,
    piola_ref, force_ref, back_ref,
    raw, far, b_all, f_all, k_all, ss, gs,
):
    blocks, lanes = weight_ref.shape
    fanout = far.shape[1]
    cap = 4
    coeff = -3.0 / math.sqrt(fanout * lanes)
    inv = 1.0 / SUPPORT_SQ
    back_ref[...] = jnp.zeros_like(back_ref)
    gs[...] = jnp.zeros_like(gs)
    raw[...] = jnp.zeros_like(raw)
    row = lax.broadcasted_iota(jnp.int32, (8, lanes), 0)

    def far_side(b, _):
        centre = centre_ref[pl.ds(pl.multiple_of(b * 8, 8), 8), :]
        for k in range(fanout):
            raw[k, 0:ROWS, :] = got_ref[pl.ds(start_ref[0, k * blocks + b], ROWS, stride=cap), :]
        for k in range(fanout):
            t = raw[k] - centre
            far[b, k] = t
            square = t * t
            norm = square[0:1] + square[1:2] + square[2:3]
            place = jnp.where(row == 3, 1.0, jnp.where(row == 7, -inv * norm, t))
            h, m, l = parts(place, 3)
            cols = pl.ds(k * lanes, lanes)
            b_all[b, :, cols] = jnp.concatenate([h, h, h, m, m, l], axis=0).astype(BF16)
            weight = raw[k, pl.ds(6, 8, stride=0), :]
            heavy = weight * jnp.where(row == 6, 1.0, t)
            feats = [heavy] + [raw[k, pl.ds(3 + a, 8, stride=0), :] * heavy for a in range(3)]
            split = [parts(v, 2) for v in feats]
            f_all[b, :, cols] = jnp.concatenate(
                [v[0] for v in split] + [v[1] for v in split], axis=0
            ).astype(BF16)
        return 0


    def forward(g, q):
        turn = g % 2
        b = g * GROUP + q
        far_side(b, 0)
        near = jnp.maximum(mm(at_ref[b], b_all[b], NN), 0.0)
        near = near * near
        hi = near.astype(BF16)
        lo = (near - hi.astype(F32)).astype(BF16)
        k_all[turn * GROUP + q, 0:lanes, :] = hi
        k_all[turn * GROUP + q, lanes:, :] = lo
        feat = f_all[b]
        sums = mm(
            jnp.concatenate([hi, lo], axis=1), jnp.concatenate([feat, feat], axis=1), NT
        )
        sums = jnp.transpose(sums)
        ss[turn, pl.ds(pl.multiple_of(q * 32, 32), 32), :] = sums[0:32] + sums[32:64]

    def middle(g):
        turn = g % 2
        rows = pl.ds(pl.multiple_of(g * GROUP, GROUP), GROUP)

        def total(f):
            return ss[turn, pl.ds(f, GROUP, stride=32), :]

        mass = total(6)
        weight = weight_ref[rows, :]
        inside = (weight > 0).astype(F32)
        here = [pos_ref[c, rows, :] for c in range(3)]
        here = [x - x[:, 0:1] for x in here]
        moved = [disp_ref[c, rows, :] for c in range(3)]
        column = [coeff * (here[c] * mass - total(c)) for c in range(3)]
        deform = [
            [
                (1.0 if a == c else 0.0)
                + coeff * (here[c] * total(3 + a) - total(8 + 8 * a + c))
                - moved[a] * column[c]
                for c in range(3)
            ]
            for a in range(3)
        ]
        strain = [[None] * 3 for _ in range(3)]
        for a in range(3):
            for c in range(a, 3):
                v = sum(deform[k][a] * deform[k][c] for k in range(3))
                strain[a][c] = strain[c][a] = 0.5 * (v - (1.0 if a == c else 0.0))
        trace = lame_ref[0, rows, :] * (strain[0][0] + strain[1][1] + strain[2][2])
        twice = 2.0 * lame_ref[1, rows, :]
        second = [
            [(trace if a == c else 0.0) + twice * strain[a][c] for c in range(3)] for a in range(3)
        ]
        scaled = [[None] * 3 for _ in range(3)]
        for a in range(3):
            for c in range(3):
                v = sum(deform[a][k] * second[k][c] for k in range(3)) * inside
                piola_ref[3 * a + c, rows, :] = v
                scaled[a][c] = weight * v
        for a in range(3):
            own = sum(scaled[a][c] * column[c] for c in range(3))
            force_ref[a, rows, :] = own
            feats = scaled[a] + [sum(scaled[a][c] * here[c] for c in range(3))]
            for f, v in enumerate(feats):
                h, l = parts(v, 2)
                gs[turn, pl.ds(f * 8 + a, GROUP, stride=32), :] = h
                gs[turn, pl.ds(f * 8 + 4 + a, GROUP, stride=32), :] = l

    def backward(g, q):
        turn = g % 2
        b = g * GROUP + q
        feat = gs[turn, pl.ds(pl.multiple_of(q * 32, 32), 32), :].astype(BF16)
        feat = jnp.concatenate([feat, feat], axis=1)
        for k in range(0, fanout, 2):
            sums = mm(feat, k_all[turn * GROUP + q, :, pl.ds(k * lanes, 2 * lanes)], NN)
            for j in range(2):
                back = [sums[8 * f : 8 * f + 8, j * lanes : (j + 1) * lanes] for f in range(4)]
                cast = [far[b, k + j, pl.ds(c, 8, stride=0), :] for c in (0, 1, 2, 6)]
                v = back[3] - sum(cast[c] * back[c] for c in range(3))
                v = (-coeff * cast[3]) * v
                first = start_ref[1, (k + j) * blocks + b]
                back_ref[pl.ds(first, 3, stride=cap), :] = v[0:3] + v[4:7]

    def first(q, _):
        forward(0, q)
        return 0

    def both(g, _):
        for q in range(2):
            forward(g, q)
        middle(g - 1)
        for q in range(2, GROUP):
            forward(g, q)
            backward(g - 1, q - 2)
        for q in range(GROUP - 2, GROUP):
            backward(g - 1, q)
        return 0

    def last(q, _):
        backward(groups - 1, q)
        return 0

    groups = blocks // GROUP
    lax.fori_loop(0, GROUP, first, 0, unroll=GROUP)
    lax.fori_loop(1, groups, both, 0, unroll=groups - 1)
    middle(groups - 1)
    lax.fori_loop(0, GROUP, last, 0, unroll=GROUP)


def returned_kernel(code_ref, got_ref, force_ref, out_ref):
    comps, blocks, lanes = force_ref.shape
    rows = got_ref.shape[0]
    target = lax.broadcasted_iota(jnp.int32, (comps * blocks, rows), 0)
    chosen = (target == code_ref[...]).astype(F32).astype(BF16)
    out = force_ref[...].reshape(comps * blocks, lanes)
    for part in parts(got_ref[...], 2):
        out = out + mm(chosen, part.astype(BF16), NN)
    out_ref[...] = out.reshape(comps, blocks, lanes)


def vmem(count):
    return [pl.BlockSpec(memory_space=pltpu.VMEM)] * count


SMEM = pl.BlockSpec(memory_space=pltpu.SMEM)
ANY = pl.BlockSpec(memory_space=pl.ANY)


def call(body, name, out, in_specs, scratch=(), kib=8192, flops=1_000_000, size=1_000_000):
    many = isinstance(out, tuple)
    return pl.pallas_call(
        body,
        out_shape=out,
        in_specs=in_specs,
        out_specs=tuple(vmem(len(out))) if many else vmem(1)[0],
        scratch_shapes=list(scratch),
        compiler_params=pltpu.CompilerParams(vmem_limit_bytes=kib * 2**10),
        cost_estimate=pl.CostEstimate(flops=flops, bytes_accessed=size, transcendentals=0),
        name=name,
    )


def main_call(start, pos_t, disp_t, weight, lame_t, at, centre, got):
    blocks, lanes = weight.shape
    fanout = start.shape[1] // blocks
    wide = fanout * lanes
    back = got.shape[0] // ROWS * 3
    return call(
        main_kernel,
        "pairs",
        (
            jax.ShapeDtypeStruct((9, blocks, lanes), F32),
            jax.ShapeDtypeStruct((3, blocks, lanes), F32),
            jax.ShapeDtypeStruct((back, lanes), F32),
        ),
        [SMEM] + vmem(7),
        [
            pltpu.VMEM((fanout, 8, lanes), F32),
            pltpu.VMEM((blocks, fanout, 8, lanes), F32),
            pltpu.VMEM((blocks, SIDE, wide), BF16),
            pltpu.VMEM((blocks, 64, wide), BF16),
            pltpu.VMEM((2 * GROUP, 2 * lanes, wide), BF16),
            pltpu.VMEM((2, GROUP * 32, lanes), F32),
            pltpu.VMEM((2, GROUP * 32, lanes), F32),
        ],
        kib=36000,
        flops=60_000_000,
        size=4_000_000,
    )(start, pos_t, disp_t, weight, lame_t, at, centre, got)


def per_device(ref_pos, disp, volume, lame, pad_count, nbr_owner, nbr_local, contact_block):
    blocks, _, lanes = ref_pos.shape
    fanout = nbr_local.shape[1]
    across = lax.axis_size("gx")
    deep = lax.axis_size("yz")
    devices = across * deep
    cap = 2 * blocks * fanout // devices
    total = blocks * fanout
    shape = jax.ShapeDtypeStruct

    ask, start = call(
        lambda *refs: plan_kernel(*refs, cap=cap),
        "plan",
        (shape((devices, 16), jnp.int32), shape((2, total), jnp.int32)),
        [ANY] * 2,
        [
            pltpu.VMEM((fanout, 1, blocks), jnp.int32),
            pltpu.VMEM((fanout, blocks), jnp.int32),
            pltpu.VMEM((8, total), jnp.int32),
            pltpu.SemaphoreType.DMA((2,)),
        ],
        kib=65472,
    )(jnp.transpose(nbr_owner, (1, 2, 0)), jnp.transpose(nbr_local))
    asked = lax.all_to_all(ask, AXES, split_axis=0, concat_axis=0, tiled=True)

    usable = (jnp.arange(lanes)[None, :] < (lanes - pad_count)[:, None]).astype(F32)
    weight = volume * usable
    pos_t = jnp.transpose(ref_pos, (1, 0, 2))
    disp_t = jnp.transpose(disp, (1, 0, 2))
    lame_t = jnp.transpose(lame, (1, 0, 2))

    surface = jnp.concatenate([ref_pos + disp, weight[:, None, :]], axis=1)
    up = [(i, i + 1) for i in range(across - 1)]
    down = [(i + 1, i) for i in range(across - 1)]
    below = lax.ppermute(surface[blocks - SH :], "gx", up)
    above = lax.ppermute(surface[:SH], "gx", down)
    local = contact_block % blocks
    row = contact_block // blocks // deep
    pick = jnp.where(row < lax.axis_index("gx"), local - (blocks - SH), SH + local)

    at, centre, data = call(
        own_kernel,
        "own",
        (
            shape((blocks, lanes, SIDE), BF16),
            shape((blocks * 8, lanes), F32),
            shape((3 * blocks, ROWS * lanes), BF16),
        ),
        vmem(3),
        [pltpu.VMEM((GROUP * SIDE, lanes), F32)],
    )(pos_t, disp_t, weight)

    picked = call(
        lambda *refs: provide_kernel(*refs, cap=cap),
        "provide",
        shape((devices * cap * ROWS, lanes), F32),
        vmem(2),
        [pltpu.VMEM((devices * cap, lanes), jnp.int32)],
    )(asked, data)
    got = lax.all_to_all(
        picked.reshape(devices, ROWS, cap, lanes), AXES, split_axis=0, concat_axis=0, tiled=True
    ).reshape(devices * cap * ROWS, lanes)

    piola, force, back = main_call(start, pos_t, disp_t, weight, lame_t, at, centre, got)
    received = lax.all_to_all(
        back.reshape(devices, 3, cap, lanes), AXES, split_axis=0, concat_axis=0, tiled=True
    )
    force = call(
        contact_kernel,
        "contact",
        shape((3, blocks, lanes), F32),
        vmem(5) + [SMEM] + vmem(1),
        [pltpu.VMEM((2 * SH, 4, lanes, lanes), F32), pltpu.VMEM((3, blocks, lanes), F32)],
        flops=20_000_000,
    )(pos_t, disp_t, weight, below, above, pick, force)
    ids = asked[:, None, 0:cap]
    code = jnp.where(ids >= 0, ids + blocks * jnp.arange(3)[None, :, None], -1).reshape(1, -1)
    force = call(returned_kernel, "returned", shape((3, blocks, lanes), F32), vmem(3))(
        code, received.reshape(devices * cap * 3, lanes), force
    )
    return (jnp.transpose(force, (1, 0, 2)), jnp.transpose(piola, (1, 0, 2)))


def solution(mesh):
    return jax.shard_map(
        per_device,
        mesh=mesh,
        in_specs=(
            P(AXES, None, None),
            P(AXES, None, None),
            P(AXES, None),
            P(AXES, None, None),
            P(AXES),
            P(AXES, None, None),
            P(AXES, None),
            P(AXES, None),
        ),
        out_specs=(P(AXES, None, None), P(AXES, None, None)),
        check_vma=False,
    )
```
